32 devices in a mesh: blk: 8 (over z, x), sub: 4 (over y, core).
Axes of the slice: x: 2, y: 2, z: 4, core: 2. Of those that a mesh axis runs over, the one named last changes fastest.
Arguments:
- rhs: float32 [150, 98304], P(None, ('blk', 'sub')), may hold values from -6 to 6
- coeff: float32 [98304], P(('blk', 'sub')), may hold values from 0.5 to 4
- s_ref: float32 [150, 150], replicated, as said below
- m_inv: float32 [150, 150], replicated, as said below
- restriction: float32 [8, 150], replicated, may hold values from -0.5 to 0.5
- partner: int32 [8, 4], P('blk'), may hold values from 0 to 7, as said below
- counts: int32 [8, 4, 4], P('blk', 'sub'), may hold values from 96 to 192, as said below
- owner: int32 [8, 4, 16], P('blk', 'sub'), may hold values from 0 to 7, as said below
- c_inv: float32 [8, 4, 512, 512], P('blk', 'sub'), as said below
Outputs:
- solution: float32 [150, 98304], P(None, ('blk', 'sub'))
The draws below stay inside these ranges and needn't reach their ends.
Inputs may be any that keep to these rules, and one draw needn't show every extreme that they name: For each direction pair (0, 1) and (2, 3) the column is a permutation of the blocks, and partner[partner[b, 0], 1] = b, partner[partner[b, 2], 3] = b. counts[b, s, k] = counts[partner[b, k], s, k xor 1]; the partition faces are those of the first counts[b, s, k] local elements. For every sub index, each owner block owns at most 64 aggregates, and some owner owns exactly 64. `s_ref`: symmetric positive definite. `m_inv`: symmetric positive definite. `c_inv`: each matrix symmetric positive definite.
All inputs are finite; a program needn't handle non-finite values.
Results may differ from the reference program's by a relative error of at most 0.00015.
Values sent between devices are 32-bit elements; how exact they have to be, the bound alone decides.
A program may use at most 128 MiB of HBM per device.

```python
import math
import jax
import jax.numpy as jnp
from jax import lax

FACE = 25
TRACE = 150
COARSE = 8
E_DEV = 3072
NRB = 16
CAP = 192
ITERS = 2
CAPO = 64
AGG = 192
EL = 98304
N_BLK = 8
N_SUB = 4


def matching(key):
    first = jax.random.permutation(jax.random.fold_in(key, 11), N_BLK).astype(jnp.int32)
    second = jax.random.permutation(jax.random.fold_in(key, 12), N_BLK).astype(jnp.int32)
    return (first, second)


def inverse_of(order):
    return jnp.zeros((N_BLK,), jnp.int32).at[order].set(jnp.arange(N_BLK, dtype=jnp.int32))


def draw_partner(key, part):
    first, second = matching(key)
    return jnp.stack([first, inverse_of(first), second, inverse_of(second)], 1).astype(jnp.int32)


def draw_counts(key, part):
    first, second = matching(key)
    even_one = jax.random.randint(jax.random.fold_in(key, 21), (N_BLK, N_SUB), CAP // 2, CAP + 1).astype(jnp.int32)
    even_two = jax.random.randint(jax.random.fold_in(key, 22), (N_BLK, N_SUB), CAP // 2, CAP + 1).astype(jnp.int32)
    even_one = even_one.at[0, 0].set(CAP)
    odd_one = even_one[inverse_of(first)]
    odd_two = even_two[inverse_of(second)]
    return jnp.stack([even_one, odd_one, even_two, odd_two], 2).astype(jnp.int32)


def symmetric(key, shape, scale):
    order = shape[-1]
    noise = jax.random.normal(key, shape, jnp.float32) * (scale / order ** 0.5)
    return (noise + jnp.swapaxes(noise, -1, -2)) * 0.7071


def draw_s_ref(key, part):
    return 1.5 * jnp.eye(TRACE, dtype=jnp.float32) + symmetric(key, (TRACE, TRACE), 0.5)


def draw_m_inv(key, part):
    return 0.5 * jnp.eye(TRACE, dtype=jnp.float32) + symmetric(key, (TRACE, TRACE), 0.2)


def draw_c_inv(key, part):
    order = COARSE * CAPO
    noise = symmetric(key, (N_BLK, N_SUB, order, order), 0.3)
    return 0.3 * (jnp.eye(order, dtype=jnp.float32)[None, None] + noise)


def draw_owner(key, part):
    busy_count = max(N_BLK // 8, 1)
    item_total = N_BLK * NRB
    rest_total = item_total - CAPO - 3 * NRB * (busy_count - 1)
    others = N_BLK - busy_count
    base_load = rest_total // others
    extra_count = rest_total - base_load * others
    owner_index = jnp.arange(N_BLK, dtype=jnp.int32)
    tail_load = base_load + (owner_index - busy_count < extra_count).astype(jnp.int32)
    owner_loads = jnp.where(owner_index == 0, CAPO, jnp.where(owner_index < busy_count, 3 * NRB, tail_load))
    load_ends = jnp.cumsum(owner_loads)
    template = jnp.searchsorted(load_ends, jnp.arange(item_total, dtype=jnp.int32), side='right').astype(jnp.int32)

    def one_sub(sub_index):
        labels = jax.random.permutation(jax.random.fold_in(key, 100 + sub_index), N_BLK).astype(jnp.int32)
        placed = labels[template]
        return jax.random.permutation(jax.random.fold_in(key, 300 + sub_index), placed)
    every_sub = jax.vmap(one_sub)(jnp.arange(N_SUB, dtype=jnp.int32))
    return jnp.transpose(every_sub.reshape(N_SUB, N_BLK, NRB), (1, 0, 2)).astype(jnp.int32)


def levels(key, shape, split, smallest, top_value):
    gain, own = 1.0, jax.random.fold_in(key, 6)
    for position, shards_of in split:
        draws = jnp.exp(jax.random.uniform(jax.random.fold_in(own, position), (shards_of,), jnp.float32, smallest / len(split), top_value / len(split)))
        gain = gain * jnp.repeat(draws, shape[position] // shards_of).reshape([-1 if axis == position else 1 for axis in range(len(shape))])
    return gain


def bell_draw(rng, extent, scale, reach, cuts=(), kind=jnp.bfloat16):
    array = scale * jax.random.normal(rng, extent, jnp.float32)
    if cuts:
        array = array * levels(rng, extent, cuts, -0.22, 0.18)
    return jnp.clip(array, -reach, reach).astype(kind)


def setup_inputs(seed: int = 0) -> dict:
    seeds = jax.random.split(jax.random.key(seed), 10)
    rhs = bell_draw(seeds[0], (TRACE, EL), 1.0, 6.0, ((1, 32),), jnp.float32)
    coeff = jnp.clip(jnp.exp(math.log(4.0) - 2.0794415 * jax.random.uniform(seeds[1], (EL,), jnp.float32) ** levels(seeds[1], (EL,), ((0, 32),), -0.2, 0.2)), 0.5, 4.0)
    s_ref = draw_s_ref(jax.random.fold_in(seeds[9], 71), 0)
    m_inv = draw_m_inv(jax.random.fold_in(seeds[9], 71), 0)
    restriction = bell_draw(seeds[4], (COARSE, TRACE), TRACE ** -0.5, 0.5, (), jnp.float32)
    partner = draw_partner(jax.random.fold_in(seeds[9], 71), 0)
    counts = draw_counts(jax.random.fold_in(seeds[9], 71), 0)
    owner = draw_owner(jax.random.fold_in(seeds[9], 71), 0)
    c_inv = draw_c_inv(jax.random.fold_in(seeds[9], 71), 0)
    return dict(rhs=rhs, coeff=coeff, s_ref=s_ref, m_inv=m_inv, restriction=restriction, partner=partner, counts=counts, owner=owner, c_inv=c_inv)


highest = lax.Precision.HIGHEST
penalty = 1.0
damping = 0.5


def neighbours(field, partner, counts):
    column = field[4 * FACE:].reshape(2 * FACE, N_BLK, N_SUB * E_DEV)
    lower_faces = column[:FACE]
    upper_faces = column[FACE:]
    zero_column = jnp.zeros((FACE, N_BLK, 1), jnp.float32)
    from_above = jnp.concatenate([lower_faces[:, :, 1:], zero_column], 2)
    from_below = jnp.concatenate([zero_column, upper_faces[:, :, :-1]], 2)
    column_rows = jnp.concatenate([from_below, from_above], 0).reshape(2 * FACE, EL)
    lateral = field[:4 * FACE].reshape(4, FACE, N_BLK, N_SUB, E_DEV)[:, :, :, :, :CAP]
    places = jnp.arange(CAP, dtype=jnp.int32)
    pieces = []
    for direction in range(4):
        source = jnp.take(lateral[direction ^ 1], partner[:, direction], axis=1)
        keep = (places[None, None, :] < counts[:, :, direction][:, :, None]).astype(jnp.float32)
        pieces.append(source * keep[None])
    sides = jnp.stack(pieces, 0)
    sides = jnp.concatenate([sides, jnp.zeros((4, FACE, N_BLK, N_SUB, E_DEV - CAP), jnp.float32)], 4)
    return jnp.concatenate([sides.reshape(4 * FACE, EL), column_rows], 0)


def operate(field, coeff, s_ref, partner, counts):
    local = jnp.dot(s_ref, field, precision=highest, preferred_element_type=jnp.float32) * coeff[None, :]
    return local + penalty * (field - neighbours(field, partner, counts))


def coarse(residual, restriction, owner, c_inv):
    projected = jnp.dot(restriction, residual, precision=highest, preferred_element_type=jnp.float32)
    summed = projected.reshape(COARSE, N_BLK, N_SUB, NRB, AGG).sum(4)
    items = jnp.transpose(summed, (2, 1, 3, 0)).reshape(N_SUB, N_BLK * NRB, COARSE)
    owners = jnp.transpose(owner, (1, 0, 2)).reshape(N_SUB, N_BLK * NRB)
    onehot = (owners[:, :, None] == jnp.arange(N_BLK, dtype=jnp.int32)[None, None, :]).astype(jnp.int32)
    ahead = jnp.cumsum(onehot, 1) - onehot
    slots = jnp.sum(onehot * ahead, 2).astype(jnp.int32)
    target = (owners * CAPO + slots).astype(jnp.int32)
    gathered = jax.vmap(lambda values, ids: jax.ops.segment_sum(values, ids, num_segments=N_BLK * CAPO))(items, target)
    gathered = gathered.reshape(N_SUB, N_BLK, CAPO * COARSE)
    solved = jnp.einsum("bsij,sbj->bsi", c_inv, gathered, precision=highest)
    solved = solved.reshape(N_BLK, N_SUB, CAPO, COARSE)
    sub_ids = jnp.arange(N_SUB, dtype=jnp.int32)[:, None]
    back = solved[owners, sub_ids, slots].reshape(N_SUB, N_BLK, NRB, COARSE)
    spread = jnp.transpose(back, (3, 1, 0, 2)).reshape(COARSE, N_BLK * N_SUB * NRB)
    prolonged = jnp.dot(restriction.T, spread, precision=highest, preferred_element_type=jnp.float32)
    return jnp.broadcast_to(prolonged[:, :, None], (TRACE, N_BLK * N_SUB * NRB, AGG)).reshape(TRACE, EL)


def reference(rhs, coeff, s_ref, m_inv, restriction, partner, counts, owner, c_inv):
    solution = jnp.zeros_like(rhs)
    for sweep in range(ITERS):
        residual = rhs - operate(solution, coeff, s_ref, partner, counts)
        local = jnp.dot(m_inv, residual, precision=highest, preferred_element_type=jnp.float32) / coeff[None, :]
        solution = solution + damping * (local + coarse(residual, restriction, owner, c_inv))
    return solution
```

```python
import functools

import jax
import jax.numpy as jnp
from jax import lax
from jax.experimental import pallas as pl
from jax.experimental.pallas import tpu as pltpu
from jax.sharding import PartitionSpec as P

FACE = 25
COARSE = 8
CAP = 192
CAPO = 64
AGG = 192
LANES = 128
PER_TILE = 4
F32 = jnp.float32
BF16 = jnp.bfloat16
HIGHEST = lax.Precision.HIGHEST


def iota(shape, dim):
    return lax.broadcasted_iota(jnp.int32, shape, dim)


def halves(x):
    high = x.astype(BF16)
    return high, (x - high.astype(F32)).astype(BF16)


def thirds(x):
    high = x.astype(BF16)
    rest = x - high.astype(F32)
    mid = rest.astype(BF16)
    return high, mid, (rest - mid.astype(F32)).astype(BF16)


def product(stacked, x):
    rows = stacked.shape[0] // 2
    high, low = halves(x)
    both = jnp.dot(stacked, high, preferred_element_type=F32)
    return both[:rows] + both[rows:] + jnp.dot(stacked[:rows], low, preferred_element_type=F32)


def nt(a, b, precision=None):
    return lax.dot_general(
        a, b, (((1,), (1,)), ((), ())), precision=precision, preferred_element_type=F32
    )


def kernel(
    blocks, subs,
    partner_hbm, counts_hbm, owner_hbm,
    rhs_hbm, coeff_hbm, s_ref_hbm, m_inv_hbm, restriction_hbm, c_inv_hbm,
    out, lift_out,
    partner_s, counts_s, owner_s, coeff, s_ref, m_inv, restriction,
    rhs, c_inv, lhs, lhs_s, rpad, field, resid, msg1, msg3, got1, got3, y_a, y_b, got_a, got_b,
    face_msg, faces, pass_msg, passed, ends, hop, got_hop,
    s1, r1, s2, r2, s3, r3, s4, r4, sf, rf, se, re, sh, rh, sp, rp, load, load_c, load_s,
):
    elements = rhs.shape[1]
    nrb = elements // AGG
    width = PER_TILE * AGG
    tiles = elements // width
    packs = blocks * nrb // LANES
    per_pack = LANES // nrb
    me = lax.axis_index("blk")
    sub = lax.axis_index("sub")
    trace = rhs.shape[0]

    loads = [
        pltpu.make_async_copy(
            rhs_hbm.at[:, pl.ds(t * width, width)], rhs.at[:, pl.ds(t * width, width)], load.at[t]
        )
        for t in range(tiles)
    ]
    small = [
        pltpu.make_async_copy(src, dst, load_s.at[i])
        for i, (src, dst) in enumerate(
            [
                (m_inv_hbm, m_inv), (restriction_hbm, restriction), (coeff_hbm, coeff),
                (s_ref_hbm, s_ref), (partner_hbm, partner_s), (counts_hbm, counts_s),
                (owner_hbm, owner_s),
            ]
        )
    ]
    for copy in small[:3] + loads + small[3:]:
        copy.start()
    load_solver = pltpu.make_async_copy(c_inv_hbm, c_inv, load_c)
    load_solver.start()
    barrier = pltpu.get_barrier_semaphore()

    def greet(i, carry):
        pl.semaphore_signal(
            barrier, inc=1, device_id={"blk": lax.rem(me + i, blocks)},
            device_id_type=pl.DeviceIdType.MESH,
        )
        return carry

    lax.fori_loop(1, blocks, greet, 0)

    @pl.when(sub > 0)
    def _():
        pl.semaphore_signal(
            barrier, inc=1, device_id={"sub": sub - 1}, device_id_type=pl.DeviceIdType.MESH
        )

    @pl.when(sub < subs - 1)
    def _():
        pl.semaphore_signal(
            barrier, inc=1, device_id={"sub": sub + 1}, device_id_type=pl.DeviceIdType.MESH
        )

    def spread(src, dst, send, recv):
        def one(i, carry):
            peer = lax.rem(me + i, blocks)
            pltpu.make_async_remote_copy(
                src_ref=src, dst_ref=dst.at[me], send_sem=send.at[peer], recv_sem=recv.at[me],
                device_id={"blk": peer}, device_id_type=pl.DeviceIdType.MESH,
            ).start()
            return carry

        lax.fori_loop(1, blocks, one, 0)

    def handle(src, dst, send, recv, peer):
        return pltpu.make_async_remote_copy(
            src_ref=src, dst_ref=dst.at[peer], send_sem=send.at[peer], recv_sem=recv.at[peer],
            device_id={"blk": peer}, device_id_type=pl.DeviceIdType.MESH,
        )

    def collect(src, dst, send, recv):
        def one(i, carry):
            handle(src, dst, send, recv, lax.rem(me + i, blocks)).wait_recv()
            return carry

        lax.fori_loop(1, blocks, one, 0)

    def sent(src, dst, send, recv):
        def one(i, carry):
            handle(src, dst, send, recv, lax.rem(me + i, blocks)).wait_send()
            return carry

        lax.fori_loop(1, blocks, one, 0)

    def beside(src, dst, slot, send, recv, peer):
        return pltpu.make_async_remote_copy(
            src_ref=src, dst_ref=dst.at[slot], send_sem=send.at[slot], recv_sem=recv.at[slot],
            device_id={"sub": peer}, device_id_type=pl.DeviceIdType.MESH,
        )

    for copy in small[:3]:
        copy.wait()
    lhs[0:trace] = m_inv[...]
    lhs[trace:152] = jnp.zeros((152 - trace, trace), F32)
    lhs[152:160] = restriction[...]
    both = lhs[...]
    high, low = halves(both)
    stack_m = jnp.concatenate([high, low], 0)
    rpad[...] = jnp.zeros((COARSE, 256), F32)
    rpad[:, 0:trace] = restriction[...]
    spread_r = rpad[...]
    backward = pltpu.roll(spread_r, 256 - FACE, 1)
    forward = pltpu.roll(spread_r, FACE, 1)
    r_lane = iota((COARSE, 256), 1)

    def at(slot, from_slot):
        moved = backward if from_slot > slot else forward
        inside = (r_lane >= slot * FACE) & (r_lane < (slot + 1) * FACE)
        return jnp.where(inside, moved, 0.0)

    low_part, high_part = at(4, 5), at(5, 4)
    sides = [at(k, k ^ 1) for k in range(4)]
    high, low = halves(jnp.concatenate(sides, 0)[:, :trace])
    stack_l = jnp.concatenate([high, low], 0)

    lane = iota((COARSE, LANES), 1)
    wide_lane = iota((COARSE, width), 1)

    def gather_lanes(values, total, tile):
        for a in range(PER_TILE):
            inside = (wide_lane >= a * AGG) & (wide_lane < (a + 1) * AGG)
            part = jnp.sum(jnp.where(inside, values, 0.0), 1, keepdims=True)
            total = jnp.where(lane == tile * PER_TILE + a, part, total)
        return total

    def spread_lanes(values, tile, rows):
        where = iota((rows, width), 1)
        first = tile * PER_TILE
        wide = jnp.broadcast_to(values[:, first + PER_TILE - 1 : first + PER_TILE], (rows, width))
        for a in range(PER_TILE - 2, -1, -1):
            wide = jnp.where(
                where < (a + 1) * AGG, values[:, first + a : first + a + 1], wide
            )
        return wide

    zero_tile = jnp.zeros((COARSE, LANES), F32)
    sums = zero_tile
    coeff_sums = zero_tile
    for tile in range(tiles):
        cols = slice(tile * width, (tile + 1) * width)
        loads[tile].wait()
        made = product(stack_m, rhs[:, cols])
        c_row = coeff[:, cols]
        field[:, LANES + tile * width : LANES + (tile + 1) * width] = made[:152] * (0.5 / c_row)
        sums = gather_lanes(made[152:160], sums, tile)
        coeff_sums = gather_lanes(
            jnp.broadcast_to(c_row, (COARSE, width)), coeff_sums, tile
        )

    def place(values):
        values = jnp.where(lane < nrb, values, 0.0)
        return pltpu.roll(values, lax.rem(me, per_pack) * nrb, 1)

    for copy in small[3:]:
        copy.wait()
    lhs_s[0:trace] = s_ref[...]
    lhs_s[trace:160] = jnp.zeros((160 - trace, trace), F32)
    high, low = halves(lhs_s[...])
    stack_s = jnp.concatenate([high, low], 0)
    side_lane = iota((COARSE, 256), 1)
    side_sums = zero_tile
    made = product(stack_l, field[0:trace, LANES : LANES + 256])
    for k in range(4):
        part = jnp.where(side_lane < counts_s[0, k], made[8 * k : 8 * k + 8], 0.0)
        side_sums = jnp.where(lane == k, jnp.sum(part, 1, keepdims=True), side_sums)
    owner_tile = zero_tile
    row8 = iota((COARSE, LANES), 0)
    for g in range(nrb):
        owner_tile = jnp.where(lane == g, owner_s[0, g].astype(F32), owner_tile)
    for k in range(4):
        owner_tile = jnp.where(
            (row8 == 1) & (lane == k), partner_s[0, k].astype(F32), owner_tile
        )
        owner_tile = jnp.where(
            (row8 == 2) & (lane == k), counts_s[0, k].astype(F32), owner_tile
        )
    owner_tile = jnp.where(row8 == 3, coeff_sums, owner_tile)
    msg1[0:8] = place(sums)
    msg1[8:16] = place(owner_tile)
    msg1[16:24] = place(side_sums)
    got1[me] = msg1[...]

    pl.semaphore_wait(
        barrier,
        blocks - 1 + (sub > 0).astype(jnp.int32) + (sub < subs - 1).astype(jnp.int32),
    )
    spread(msg1, got1, s1, r1)

    lines = blocks // 2
    line = me // 2
    side = lax.rem(me, 2)
    mate = me + 1 - 2 * side
    head = field[0:104, LANES : 2 * LANES]
    tail = field[0:104, 2 * LANES : 3 * LANES]
    half = iota((56, LANES), 1) < LANES // 2
    turned = pltpu.roll(tail, LANES // 2, 1)
    upper = jnp.concatenate([turned[56:104], jnp.zeros((8, LANES), F32)], 0)
    face_msg[0:104] = head
    face_msg[104:160] = jnp.where(half, tail[0:56], upper)
    faces[line] = face_msg[...]

    def face_copy(place_at, peer):
        return pltpu.make_async_remote_copy(
            src_ref=face_msg, dst_ref=faces.at[place_at], send_sem=sf.at[peer],
            recv_sem=rf.at[place_at], device_id={"blk": peer * 2 + side},
            device_id_type=pl.DeviceIdType.MESH,
        )

    def send_faces(offset):
        face_copy(line, lax.rem(line + offset, lines)).start()

    pass_copy = pltpu.make_async_remote_copy(
        src_ref=pass_msg, dst_ref=passed, send_sem=sp, recv_sem=rp,
        device_id={"blk": mate}, device_id_type=pl.DeviceIdType.MESH,
    )
    first_src = field.at[96:152, LANES : 2 * LANES]
    last_src = field.at[96:152, elements : elements + LANES]

    @pl.when(sub < subs - 1)
    def _():
        beside(last_src, ends, 0, se, re, sub + 1).start()

    @pl.when(sub > 0)
    def _():
        beside(first_src, ends, 1, se, re, sub - 1).start()

    early = [1, lines - 1] if lines > 2 else [1]
    for offset in early:
        send_faces(offset)

    row56 = iota((56, width), 0)

    def second(tile, total):
        cols = slice(tile * width, (tile + 1) * width)
        u = field[:, LANES + tile * width : LANES + (tile + 1) * width]
        su = product(stack_s, u[:trace])
        c_row = coeff[:, cols]
        resid[0:trace] = rhs[:, cols] - su[:trace] * c_row - u[:trace]
        wide = field[96:152, tile * width : (tile + 1) * width + 2 * LANES]
        span = width + 2 * LANES
        below = pltpu.roll(wide, 1, 1)[:, LANES : LANES + width]
        above = pltpu.roll(wide, span - 1, 1)[:, LANES : LANES + width]
        below = pltpu.roll(below, 56 - FACE, 0)
        above = pltpu.roll(above, FACE, 0)
        column = jnp.where(
            (row56 >= 4) & (row56 < 4 + FACE), below,
            jnp.where((row56 >= 4 + FACE) & (row56 < 4 + 2 * FACE), above, 0.0),
        )
        resid[96:152] = resid[96:152] + column
        made = product(stack_m, resid[0:trace])
        out[:, cols] = u[:trace] + made[:trace] * (0.5 / c_row)
        return gather_lanes(made[152:160], total, tile)

    sums_two = zero_tile
    for tile in range(1, tiles - 1):
        sums_two = second(tile, sums_two)

    @pl.when(sub > 0)
    def _():
        beside(last_src, ends, 0, se, re, sub - 1).wait_recv()
        field[96:152, 0:LANES] = ends[0]

    @pl.when(sub == 0)
    def _():
        field[96:152, 0:LANES] = jnp.zeros((56, LANES), F32)

    @pl.when(sub < subs - 1)
    def _():
        beside(first_src, ends, 1, se, re, sub + 1).wait_recv()
        field[96:152, LANES + elements : 2 * LANES + elements] = ends[1]

    @pl.when(sub == subs - 1)
    def _():
        field[96:152, LANES + elements : 2 * LANES + elements] = jnp.zeros((56, LANES), F32)

    sums_two = second(tiles - 1, sums_two)

    collect(msg1, got1, s1, r1)

    def packed(got):
        return [
            jnp.sum(got[t * per_pack : (t + 1) * per_pack], 0) for t in range(packs)
        ]

    first_pack = packed(got1)
    owner_rows = [p[8:9] for p in first_pack]
    eye = iota((LANES, LANES), 0) == iota((LANES, LANES), 1)
    earlier = iota((LANES, LANES), 0) < iota((LANES, LANES), 1)
    owner_cols = [
        jnp.sum(jnp.where(eye, row, 0.0), 1, keepdims=True) for row in owner_rows
    ]
    slot_rows = []
    for t in range(packs):
        slot = jnp.zeros((1, LANES), F32)
        for before in range(t + 1):
            same = owner_cols[before] == owner_rows[t]
            if before == t:
                same = same & earlier
            slot = slot + jnp.sum(jnp.where(same, 1.0, 0.0), 0, keepdims=True)
        slot_rows.append(slot)
    order = COARSE * CAPO
    slot_of = (iota((order, LANES), 0) // COARSE).astype(F32)
    me_real = me.astype(F32)
    slotted = [jnp.where(slot_of == slot_rows[t], 1.0, 0.0).astype(BF16) for t in range(packs)]
    chosen = [
        jnp.where((slot_of == slot_rows[t]) & (owner_rows[t] == me_real), 1.0, 0.0).astype(BF16)
        for t in range(packs)
    ]
    pick = lax.rem(iota((order, 3 * COARSE), 0), COARSE) == lax.rem(
        iota((order, 3 * COARSE), 1), COARSE
    )

    def solve(packs_of):
        wide = jnp.zeros((order, 3 * COARSE), F32)
        for t in range(packs):
            wide = wide + nt(chosen[t], jnp.concatenate(thirds(packs_of[t]), 0))
        column = jnp.sum(jnp.where(pick, wide, 0.0), 1, keepdims=True)
        return jnp.sum(c_inv[...] * column, 0, keepdims=True)

    load_solver.wait()
    y_a[...] = solve([p[0:8] for p in first_pack])
    got_a[me] = y_a[...]
    spread(y_a, got_a, s2, r2)

    target = jnp.where(lane < nrb, me * nrb + lane, -1)
    for k in range(4):
        target = jnp.where(lane == nrb + k, partner_s[0, k] * nrb, target)
    found = jnp.zeros((COARSE, LANES), F32)
    own_sel = []
    toward = jnp.full((COARSE, LANES), -1, jnp.int32)
    for k in range(4):
        toward = jnp.where(lane == k, partner_s[0, k] * nrb + (k ^ 1), toward)
    side_found = jnp.zeros((3 * COARSE, LANES), F32)
    for t in range(packs):
        sel = iota((LANES, LANES), 0) + t * LANES == toward[0:1]
        side_found = side_found + jnp.dot(
            jnp.concatenate(thirds(first_pack[t][16:24]), 0),
            jnp.where(sel, 1.0, 0.0).astype(BF16), preferred_element_type=F32,
        )
    side_found = side_found[0:8] + side_found[8:16] + side_found[16:24]
    sides_in = jnp.sum(jnp.where(lane < 4, side_found, 0.0), 1, keepdims=True)
    sums_two = second(0, sums_two)
    sums_two = sums_two + jnp.where(lane == 0, sides_in, 0.0)
    msg3[...] = place(sums_two)
    got3[me] = msg3[...]
    spread(msg3, got3, s3, r3)
    for offset in range(2, lines - 1):
        send_faces(offset)

    base = jnp.concatenate(
        [nt(restriction[...], s_ref[...], HIGHEST)]
        + [
            part[:, :trace]
            for part in [spread_r - low_part - high_part, low_part, high_part] + sides
        ],
        0,
    )
    unit = jnp.where(iota((152, trace), 0) == iota((152, trace), 1), 1.0, 0.0)
    lifted = nt(
        unit,
        jnp.concatenate([restriction[...], jnp.zeros((7 * COARSE, trace), F32)], 0),
        HIGHEST,
    )
    weights = nt(both, base, HIGHEST)
    signs = jnp.where(iota((152, 8 * COARSE), 1) < 4 * COARSE, -0.5, 0.5)
    correct = lifted + weights[:152] * signs
    high, low = halves(correct)
    stack_x = jnp.concatenate([high, low], 0)
    reduced = weights[152:160]

    for t in range(packs):
        sel = iota((LANES, LANES), 0) + t * LANES == target[0:1]
        own_sel.append(jnp.where(sel, 1.0, 0.0).astype(BF16))
        pair = jnp.where(row8 == 0, owner_rows[t], slot_rows[t])
        found = found + jnp.dot(
            pair.astype(BF16), own_sel[t], preferred_element_type=F32
        )
    owner_sel, slot_sel = found[0:1], found[1:2]
    back = jnp.where(slot_of == slot_sel, 1.0, 0.0).astype(BF16)
    block_of = iota((blocks, COARSE, LANES), 0).astype(F32)
    keep_row = (
        iota((blocks, COARSE, order), 1) == lax.rem(iota((blocks, COARSE, order), 2), COARSE)
    )

    def rows_of(got):
        rows = jnp.where(keep_row, got[...], 0.0).reshape(blocks * COARSE, order)
        return jnp.concatenate(thirds(rows), 0)

    def fetch(rows, at_slot, owner_row):
        made = jnp.dot(rows, at_slot, preferred_element_type=F32)
        count = blocks * COARSE
        made = made[:count] + made[count : 2 * count] + made[2 * count :]
        made = made.reshape(blocks, COARSE, LANES)
        return jnp.sum(jnp.where(block_of == owner_row[None], made, 0.0), 0)

    def picked(values, onehots):
        count = values[0].shape[0]
        total = jnp.zeros((3 * count, LANES), F32)
        for value, onehot in zip(values, onehots):
            total = total + jnp.dot(
                jnp.concatenate(thirds(value), 0), onehot, preferred_element_type=F32
            )
        return total[:count] + total[count : 2 * count] + total[2 * count :]

    in_block = lax.rem(lane, nrb)
    side_sel = [
        [
            jnp.where(
                (iota((LANES, LANES), 0) + source * LANES).astype(F32)
                == first_pack[t][9:10] * float(nrb),
                1.0, 0.0,
            ).astype(BF16)
            for source in range(packs)
        ]
        for t in range(packs)
    ]

    collect(y_a, got_a, s2, r2)
    rows = rows_of(got_a)
    omegas = [0.5 * fetch(rows, slotted[t], owner_rows[t]) for t in range(packs)]
    for t in range(packs):
        hop[t] = omegas[t]

    @pl.when(sub < subs - 1)
    def _():
        beside(hop, got_hop, 0, sh, rh, sub + 1).start()

    @pl.when(sub > 0)
    def _():
        beside(hop, got_hop, 1, sh, rh, sub - 1).start()

    crossed = [picked(omegas, side_sel[t]) for t in range(packs)]

    @pl.when(sub > 0)
    def _():
        beside(hop, got_hop, 0, sh, rh, sub - 1).wait_recv()

    @pl.when(sub == 0)
    def _():
        got_hop[0] = jnp.zeros((packs, COARSE, LANES), F32)

    @pl.when(sub < subs - 1)
    def _():
        beside(hop, got_hop, 1, sh, rh, sub + 1).wait_recv()

    @pl.when(sub == subs - 1)
    def _():
        got_hop[1] = jnp.zeros((packs, COARSE, LANES), F32)

    collect(msg3, got3, s3, r3)
    base_sums = packed(got3)
    states = []
    seconds = []
    for t in range(packs):
        omega = omegas[t]
        before = jnp.where(
            in_block == 0,
            pltpu.roll(got_hop[0, t], LANES - (nrb - 1), 1), pltpu.roll(omega, 1, 1),
        )
        after = jnp.where(
            in_block == nrb - 1,
            pltpu.roll(got_hop[1, t], nrb - 1, 1), pltpu.roll(omega, LANES - 1, 1),
        )
        step_down = omega - before
        step_up = omega - after
        values = [omega * first_pack[t][11:12], float(AGG) * omega, step_down, step_up]
        share = crossed[t] * (-first_pack[t][10:11])
        for k in range(4):
            moved = share if k == 0 else pltpu.roll(share, LANES - k, 1)
            values.append(jnp.where(in_block == 0, moved, 0.0))
        change = jnp.dot(
            reduced, jnp.concatenate(values, 0), precision=HIGHEST, preferred_element_type=F32
        )
        seconds.append(base_sums[t] - change)
        states.append(jnp.concatenate([omega, step_down, step_up], 0))
    y_b[...] = solve(seconds)
    got_b[me] = y_b[...]
    spread(y_b, got_b, s4, r4)

    state = picked(states, own_sel)
    omega, step_down, step_up = state[0:8], state[8:16], state[16:24]
    across = [omega[:, nrb + k : nrb + k + 1] for k in range(4)]

    packed_row = iota((160, LANES), 0)
    face_row = jnp.where(
        packed_row < 104, packed_row,
        jnp.where(iota((160, LANES), 1) < LANES // 2, packed_row - 104, packed_row - 48),
    )

    def sources(of):
        wanted = jnp.full((160, LANES), -1.0, F32)
        for q in range(4):
            inside = (face_row >= q * FACE) & (face_row < (q + 1) * FACE)
            wanted = jnp.where(inside, of[q ^ 1], wanted)
        return wanted

    side_real = side.astype(F32)

    def from_line(wanted, start):
        for z in range(lines):
            start = jnp.where(wanted == 2.0 * z + side_real, faces[z], start)
        return start

    for offset in range(1, lines):
        face_copy(lax.rem(line + offset, lines), lax.rem(line + offset, lines)).wait_recv()
    mates = []
    for k in range(4):
        total = jnp.zeros((1, 1), F32)
        for t in range(packs):
            here = lane[0:1] + t * LANES == mate * nrb + k
            total = total + jnp.sum(
                jnp.where(here, first_pack[t][9:10], 0.0), 1, keepdims=True
            )
        mates.append(total)
    pass_msg[...] = from_line(sources(mates), jnp.zeros((160, LANES), F32))
    pass_copy.start()

    def lateral_change():
        pass_copy.wait_recv()
        wanted = sources([partner_s[0, k].astype(F32) for k in range(4)])
        taken = from_line(wanted, passed[...])
        unfolded = taken[104:160]
        turned = pltpu.roll(unfolded, LANES // 2, 1)
        wide = jnp.concatenate(
            [taken[0:104], jnp.concatenate([unfolded, turned[0:48]], 0)], 1
        )
        backward = pltpu.roll(wide, 104 - FACE, 0)
        forward = pltpu.roll(wide, FACE, 0)
        row = iota((104, 256), 0)
        col = iota((104, 256), 1)
        lateral = jnp.zeros((104, 256), F32)
        for k in range(4):
            inside = (row >= k * FACE) & (row < (k + 1) * FACE) & (col < counts_s[0, k])
            lateral = jnp.where(inside, backward if k % 2 == 0 else forward, lateral)
        made = product(stack_m[:, :104], lateral)
        out[:, 0:256] = out[:, 0:256] + made[:trace] * (0.5 / coeff[:, 0:256])

    def coarse_change(tile):
        cols = slice(tile * width, (tile + 1) * width)
        inverse = 1.0 / coeff[:, cols]
        step = lax.rem(wide_lane, AGG)
        here = spread_lanes(omega, tile, COARSE)
        scaled = here * inverse
        down = jnp.where(step == 0, spread_lanes(step_down, tile, COARSE) * inverse, 0.0)
        up = jnp.where(step == AGG - 1, spread_lanes(step_up, tile, COARSE) * inverse, 0.0)
        rows = [here, scaled, down, up]
        if tile == 0:
            for k in range(4):
                rows.append(jnp.where(wide_lane < counts_s[0, k], across[k] * inverse, 0.0))
            made = product(stack_x, jnp.concatenate(rows, 0))
        else:
            made = product(stack_x[:, : 4 * COARSE], jnp.concatenate(rows, 0))
        out[:, cols] = out[:, cols] + made[:trace]

    for tile in range(1, tiles):
        coarse_change(tile)
    coarse_change(0)
    lateral_change()

    sent(msg1, got1, s1, r1)
    for offset in range(1, lines):
        face_copy(line, lax.rem(line + offset, lines)).wait_send()
    pass_copy.wait_send()
    sent(y_a, got_a, s2, r2)
    sent(msg3, got3, s3, r3)

    @pl.when(sub < subs - 1)
    def _():
        beside(last_src, ends, 0, se, re, sub + 1).wait_send()
        beside(hop, got_hop, 0, sh, rh, sub + 1).wait_send()

    @pl.when(sub > 0)
    def _():
        beside(first_src, ends, 1, se, re, sub - 1).wait_send()
        beside(hop, got_hop, 1, sh, rh, sub - 1).wait_send()

    collect(y_b, got_b, s4, r4)
    final = 0.5 * fetch(rows_of(got_b), back, owner_sel)
    lift_out[...] = jnp.dot(
        lifted[:, 0:COARSE], final, precision=HIGHEST, preferred_element_type=F32
    )
    sent(y_b, got_b, s4, r4)


def finish(lift, held, out_hbm, done, store):
    rows, elements = held.shape
    width = 2 * AGG
    tiles = elements // width
    stores = []
    for t in range(tiles):
        cols = pl.ds(t * width, width)
        stores.append(pltpu.make_async_copy(done.at[:, cols], out_hbm.at[:, cols], store.at[t]))
    split = iota((rows, LANES), 1) < LANES // 2
    for t in range(tiles):
        first = jnp.broadcast_to(lift[:rows, 2 * t : 2 * t + 1], (rows, LANES))
        second = jnp.broadcast_to(lift[:rows, 2 * t + 1 : 2 * t + 2], (rows, LANES))
        left, mid, right = (pl.ds(t * width + q * LANES, LANES) for q in range(3))
        done[:, left] = held[:, left] + first
        done[:, mid] = held[:, mid] + jnp.where(split, first, second)
        done[:, right] = held[:, right] + second
        stores[t].start()
    for copy in stores:
        copy.wait()


def per_device(blocks, subs, rhs, coeff, s_ref, m_inv, restriction, partner, counts, owner, c_inv):
    trace, elements = rhs.shape
    width = PER_TILE * AGG
    order = COARSE * CAPO
    vmem = pl.BlockSpec(memory_space=pltpu.VMEM)
    packs = blocks * owner.shape[2] // LANES
    far = pl.BlockSpec(memory_space=pltpu.HBM)
    dma = pltpu.SemaphoreType.DMA
    held, lift = pl.pallas_call(
        functools.partial(kernel, blocks, subs),
        out_shape=(
            pltpu.VMEM((trace, elements), F32),
            pltpu.VMEM((152, LANES), F32),
        ),
        in_specs=[far] * 9,
        out_specs=(vmem, vmem),
        scratch_shapes=[
            pltpu.SMEM((1, 4), jnp.int32),
            pltpu.SMEM((1, 4), jnp.int32),
            pltpu.SMEM((1, owner.shape[2]), jnp.int32),
            pltpu.VMEM((1, elements), F32),
            pltpu.VMEM((trace, trace), F32),
            pltpu.VMEM((trace, trace), F32),
            pltpu.VMEM((COARSE, trace), F32),
            pltpu.VMEM((trace, elements), F32),
            pltpu.VMEM((order, order), F32),
            pltpu.VMEM((160, trace), F32),
            pltpu.VMEM((160, trace), F32),
            pltpu.VMEM((8, 256), F32),
            pltpu.VMEM((152, elements + 2 * LANES), F32),
            pltpu.VMEM((152, width), F32),
            pltpu.VMEM((24, LANES), F32),
            pltpu.VMEM((8, LANES), F32),
            pltpu.VMEM((blocks, 24, LANES), F32),
            pltpu.VMEM((blocks, 8, LANES), F32),
            pltpu.VMEM((1, order), F32),
            pltpu.VMEM((1, order), F32),
            pltpu.VMEM((blocks, 1, order), F32),
            pltpu.VMEM((blocks, 1, order), F32),
            pltpu.VMEM((160, LANES), F32),
            pltpu.VMEM((blocks // 2, 160, LANES), F32),
            pltpu.VMEM((160, LANES), F32),
            pltpu.VMEM((160, LANES), F32),
            pltpu.VMEM((2, 56, LANES), F32),
            pltpu.VMEM((packs, 8, LANES), F32),
            pltpu.VMEM((2, packs, 8, LANES), F32),
        ]
        + [dma((blocks,))] * 8
        + [dma((blocks // 2,))] * 2
        + [dma((2,))] * 4
        + [dma, dma, dma((elements // width,)), dma, dma((7,))],
        compiler_params=pltpu.CompilerParams(
            collective_id=0, has_side_effects=True
        ),
    )(
        partner, counts[0], owner[0], rhs, coeff[None, :], s_ref, m_inv, restriction, c_inv[0, 0],
    )
    pairs = elements // (2 * AGG)
    return pl.pallas_call(
        finish,
        out_shape=jax.ShapeDtypeStruct((trace, elements), F32),
        in_specs=[vmem, vmem],
        out_specs=far,
        scratch_shapes=[
            pltpu.VMEM((trace, elements), F32),
            dma((pairs,)),
        ],
    )(*[pltpu.with_memory_space_constraint(v, pltpu.VMEM) for v in (lift, held)])


def solution(mesh):
    in_specs = (
        P(None, ("blk", "sub")),
        P(("blk", "sub")),
        P(),
        P(),
        P(),
        P("blk", None),
        P("blk", "sub", None),
        P("blk", "sub", None),
        P("blk", "sub", None, None),
    )
    out_specs = P(None, ("blk", "sub"))
    body = functools.partial(per_device, mesh.shape["blk"], mesh.shape["sub"])
    return jax.shard_map(
        body, mesh=mesh, in_specs=in_specs, out_specs=out_specs, check_vma=False
    )
```

```python
import functools

import jax
import jax.numpy as jnp
from jax import lax
from jax.experimental import pallas as pl
from jax.experimental.pallas import tpu as pltpu
from jax.sharding import PartitionSpec as P

FACE = 25
COARSE = 8
CAP = 192
CAPO = 64
AGG = 192
LANES = 128
PER_TILE = 4
PAD = 160
PIECE = 32
QUAD = 4
WIDE = 3 * PAD
F32 = jnp.float32
BF16 = jnp.bfloat16
HIGHEST = lax.Precision.HIGHEST
MESH = pl.DeviceIdType.MESH


def iota(shape, dim):
    return lax.broadcasted_iota(jnp.int32, shape, dim)


def halves(x):
    high = x.astype(BF16)
    return high, (x - high.astype(F32)).astype(BF16)


def stacked_left(x, block, width):
    rows, lanes = x.shape
    if lanes < width:
        x = jnp.concatenate([x, jnp.zeros((rows, width - lanes), F32)], 1)
    high = x.astype(BF16).astype(F32)
    low = x - high
    return (high + pltpu.roll(high, block, 1) + pltpu.roll(low, 2 * block, 1)).astype(BF16)


def stacked_right(x):
    high, low = halves(x)
    return jnp.concatenate([high, low, high], 0)


def dot(a, b):
    return jnp.dot(a, b, preferred_element_type=F32)


def nt(a, b, precision=None):
    return lax.dot_general(
        a, b, (((1,), (1,)), ((), ())), precision=precision, preferred_element_type=F32
    )


def kernel(
    blocks, subs,
    partner_hbm, counts_hbm, owner_hbm,
    rhs_hbm, coeff_hbm, s_ref_hbm, m_inv_hbm, restriction_hbm, c_inv_hbm,
    out, lift_out,
    partner_s, counts_s, owner_s, coeff, s_ref, m_inv, restriction, rpad,
    rhs, split, c_inv, lhs, lhs_s, left_m, left_s, field, resid, tall,
    msg1, msg3, got1, got3, y_a, y_b, got_a, got_b, edge, got_edge,
    face_msg, faces, pass_msg, passed, ends,
    s1, r1, s2, r2, s3, r3, s4, r4, sx, rx, sf, rf, se, re, sp, rp, load, load_c, load_s,
):
    elements = rhs.shape[1]
    trace = m_inv.shape[0]
    nrb = elements // AGG
    width = PER_TILE * AGG
    tiles = elements // width
    packs = blocks * nrb // LANES
    per_pack = LANES // nrb
    edge_lanes = edge.shape[1]
    me = lax.axis_index("blk")
    sub = lax.axis_index("sub")
    has_below = (sub > 0).astype(jnp.int32)
    has_above = (sub < subs - 1).astype(jnp.int32)
    rising = (me * 2 < blocks).astype(jnp.int32)

    def every(j):
        return rising * (blocks - 1 - j) + (1 - rising) * j

    def other(j):
        down = blocks - 1 - j
        down = down - (down <= me).astype(jnp.int32)
        up = j + (j >= me).astype(jnp.int32)
        return rising * down + (1 - rising) * up

    barrier = pltpu.get_barrier_semaphore()

    def greet(j, carry):
        pl.semaphore_signal(barrier, inc=1, device_id={"blk": other(j)}, device_id_type=MESH)
        return carry

    lax.fori_loop(0, blocks - 1, greet, 0)

    @pl.when(sub > 0)
    def _():
        pl.semaphore_signal(barrier, inc=1, device_id={"sub": sub - 1}, device_id_type=MESH)

    @pl.when(sub < subs - 1)
    def _():
        pl.semaphore_signal(barrier, inc=1, device_id={"sub": sub + 1}, device_id_type=MESH)

    small = [
        pltpu.make_async_copy(src, dst, load_s.at[i])
        for i, (src, dst) in enumerate(
            [
                (restriction_hbm, restriction), (owner_hbm, owner_s),
                (partner_hbm, partner_s), (counts_hbm, counts_s), (coeff_hbm, coeff),
                (m_inv_hbm, m_inv), (s_ref_hbm, s_ref),
            ]
        )
    ]
    loads = [
        pltpu.make_async_copy(
            rhs_hbm.at[:, pl.ds(t * width, width)],
            rhs.at[:, pl.ds(t * width, width)], load.at[t],
        )
        for t in range(tiles)
    ]
    load_solver = pltpu.make_async_copy(c_inv_hbm, c_inv, load_c)
    for copy in small[:5] + loads + small[5:]:
        copy.start()
    load_solver.start()

    def spread(src, dst, send, recv):
        def one(j, carry):
            peer = other(j)
            pltpu.make_async_remote_copy(
                src_ref=src, dst_ref=dst.at[me], send_sem=send.at[peer], recv_sem=recv.at[me],
                device_id={"blk": peer}, device_id_type=MESH,
            ).start()
            return carry

        lax.fori_loop(0, blocks - 1, one, 0)

    def handle(src, dst, send, recv, peer):
        return pltpu.make_async_remote_copy(
            src_ref=src, dst_ref=dst.at[peer], send_sem=send.at[peer], recv_sem=recv.at[peer],
            device_id={"blk": peer}, device_id_type=MESH,
        )

    def collect(src, dst, send, recv):
        def one(j, carry):
            handle(src, dst, send, recv, lax.rem(me + j, blocks)).wait_recv()
            return carry

        lax.fori_loop(1, blocks, one, 0)

    def sent(src, dst, send, recv):
        def one(j, carry):
            handle(src, dst, send, recv, lax.rem(me + j, blocks)).wait_send()
            return carry

        lax.fori_loop(1, blocks, one, 0)

    def beside(src, dst, slot, send, recv, peer):
        return pltpu.make_async_remote_copy(
            src_ref=src, dst_ref=dst.at[slot], send_sem=send.at[slot], recv_sem=recv.at[slot],
            device_id={"sub": peer}, device_id_type=MESH,
        )

    def edge_copy(slot, place_at, peer, peer_sub):
        return pltpu.make_async_remote_copy(
            src_ref=edge, dst_ref=got_edge.at[slot, place_at],
            send_sem=sx.at[slot, peer], recv_sem=rx.at[slot, place_at],
            device_id={"blk": peer, "sub": peer_sub}, device_id_type=MESH,
        )

    lane = iota((COARSE, LANES), 1)
    left_half = lane < LANES // 2
    zero_tile = jnp.zeros((COARSE, LANES), F32)

    def lane_sums(values, total, tile):
        for p in range(PER_TILE // 2):
            first, mid, last = (
                values[:, (3 * p + q) * LANES : (3 * p + q + 1) * LANES] for q in range(3)
            )
            even = first + jnp.where(left_half, mid, 0.0)
            odd = last + jnp.where(left_half, 0.0, mid)
            at = tile * PER_TILE + 2 * p
            total = jnp.where(lane == at, jnp.sum(even, 1, keepdims=True), total)
            total = jnp.where(lane == at + 1, jnp.sum(odd, 1, keepdims=True), total)
        return total

    def lane_picks(values, total, tile, offset):
        for a in range(PER_TILE):
            at = a * AGG + offset
            total = jnp.where(lane == tile * PER_TILE + a, values[:, at : at + 1], total)
        return total

    rpad[...] = jnp.zeros((COARSE, 2 * LANES), F32)
    for row in (0, PAD):
        split[row + trace : row + PAD] = jnp.zeros((PAD - trace, width), BF16)
    resid[trace:PAD] = jnp.zeros((PAD - trace, width), F32)
    tall[trace:PAD] = jnp.zeros((PAD - trace, LANES), F32)
    small[0].wait()
    r_lane = iota((COARSE, 2 * LANES), 1)
    rpad[:, 0:trace] = restriction[...]
    spread_r = rpad[...]
    left_r = stacked_left(spread_r, PAD, 4 * LANES)[:, :WIDE]

    row8 = iota((COARSE, LANES), 0)

    def place(values):
        values = jnp.where(lane < nrb, values, 0.0)
        return pltpu.roll(values, lax.rem(me, per_pack) * nrb, 1)

    def split_tile(cols):
        high, low = halves(rhs[:, cols])
        split[0:trace] = high
        split[PAD : PAD + trace] = low
        high = split[0:PAD]
        return jnp.concatenate([high, split[PAD : 2 * PAD], high], 0)

    def describe():
        coeff_sums = zero_tile
        for tile in range(tiles):
            c_row = jnp.broadcast_to(coeff[:, tile * width : (tile + 1) * width], (COARSE, width))
            coeff_sums = lane_sums(c_row, coeff_sums, tile)
        owner_tile = zero_tile
        for g in range(nrb):
            owner_tile = jnp.where(lane == g, owner_s[0, g].astype(F32), owner_tile)
        for k in range(4):
            owner_tile = jnp.where(
                (row8 == 1) & (lane == k), partner_s[0, k].astype(F32), owner_tile
            )
            owner_tile = jnp.where(
                (row8 == 2) & (lane == k), counts_s[0, k].astype(F32), owner_tile
            )
        owner_tile = jnp.where(row8 == 3, coeff_sums, owner_tile)
        msg1[8:16] = place(owner_tile)

    tall_lane = iota((trace, LANES), 1)
    tall_left = tall_lane < LANES // 2
    totals = jnp.zeros((trace, LANES), F32)
    for tile in range(tiles):
        loads[tile].wait()
        for p in range(PER_TILE // 2):
            first, mid, last = (
                rhs[:, tile * width + (3 * p + q) * LANES : tile * width + (3 * p + q + 1) * LANES]
                for q in range(3)
            )
            even = first + jnp.where(tall_left, mid, 0.0)
            odd = last + jnp.where(tall_left, 0.0, mid)
            at = tile * PER_TILE + 2 * p
            totals = jnp.where(tall_lane == at, jnp.sum(even, 1, keepdims=True), totals)
            totals = jnp.where(tall_lane == at + 1, jnp.sum(odd, 1, keepdims=True), totals)
        if tile == max(tiles - 2, 0):
            for copy in small[1:5]:
                copy.wait()
            describe()
    tall[0:trace] = totals
    sums = dot(left_r, stacked_right(tall[...]))
    msg1[0:8] = place(sums)
    got1[me] = msg1[...]

    pl.semaphore_wait(barrier, blocks - 1 + has_below + has_above)
    spread(msg1, got1, s1, r1)

    backward = pltpu.roll(spread_r, 2 * LANES - FACE, 1)
    forward = pltpu.roll(spread_r, FACE, 1)

    def at_slot(slot, from_slot):
        moved = backward if from_slot > slot else forward
        inside = (r_lane >= slot * FACE) & (r_lane < (slot + 1) * FACE)
        return jnp.where(inside, moved, 0.0)

    low_part, high_part = at_slot(4, 5), at_slot(5, 4)
    sides = [at_slot(k, k ^ 1) for k in range(4)]
    for copy in small[5:]:
        copy.wait()
    for ref, src in ((lhs, m_inv), (lhs_s, s_ref)):
        ref[...] = jnp.zeros((PAD, 2 * LANES), F32)
        ref[0:trace, 0:trace] = src[...]
    left_m[0:PAD] = stacked_left(lhs[...], PAD, 4 * LANES)
    base = jnp.concatenate(
        [dot(left_r, stacked_right(lhs_s[...]))]
        + [spread_r - low_part - high_part, low_part, high_part] + sides,
        0,
    )
    moved = dot(stacked_left(base, PAD, 4 * LANES)[:, :WIDE], stacked_right(lhs[...]))
    left_m[PAD : PAD + 8 * COARSE] = stacked_left(moved, PAD, 4 * LANES)
    lhs[152:160] = spread_r

    groups = blocks // QUAD
    group = me // QUAD
    spot = lax.rem(me, QUAD)

    def face_copy(place_at, to, rows=slice(None)):
        return pltpu.make_async_remote_copy(
            src_ref=face_msg.at[rows], dst_ref=faces.at[place_at, rows], send_sem=sf.at[to],
            recv_sem=rf.at[place_at], device_id={"blk": group * QUAD + to}, device_id_type=MESH,
        )

    def pass_copy(place_at, to):
        return pltpu.make_async_remote_copy(
            src_ref=pass_msg.at[to], dst_ref=passed.at[place_at], send_sem=sp.at[to],
            recv_sem=rp.at[place_at], device_id={"blk": to * QUAD + spot}, device_id_type=MESH,
        )

    queue = [(step, piece) for piece in range(160 // PIECE) for step in range(1, QUAD)]

    def pace(count):
        for _ in range(min(count, len(queue))):
            step, piece = queue.pop(0)
            rows = pl.ds(piece * PIECE, PIECE)
            face_copy(spot, lax.rem(spot + step, QUAD), rows).start()

    first_src = field.at[96:152, LANES : 2 * LANES]
    last_src = field.at[96:152, elements : elements + LANES]

    less = zero_tile
    firsts = zero_tile
    lasts = zero_tile
    side_sums = zero_tile
    for tile in [0, tiles - 1] + list(range(1, tiles - 1)):
        cols = slice(tile * width, (tile + 1) * width)
        rows = PAD + (8 if tile == 0 else 4) * COARSE
        made = dot(left_m[0:rows, 0:WIDE], split_tile(cols))
        scale = 0.5 / coeff[:, cols]
        field[:, LANES + tile * width : LANES + (tile + 1) * width] = made[:PAD] * scale
        parts = [made[PAD + 8 * i : PAD + 8 * i + 8] for i in range((rows - PAD) // COARSE)]
        less = lane_sums(0.5 * parts[0] + parts[1] * scale, less, tile)
        firsts = lane_picks(parts[2] * scale, firsts, tile, 0)
        lasts = lane_picks(parts[3] * scale, lasts, tile, AGG - 1)
        if tile == 0:
            side_lane = iota((COARSE, 2 * LANES), 1)
            for k in range(4):
                part = parts[4 + k][:, : 2 * LANES] * scale[:, : 2 * LANES]
                part = jnp.where(side_lane < counts_s[0, k], part, 0.0)
                side_sums = jnp.where(lane == k, jnp.sum(part, 1, keepdims=True), side_sums)
            head = field[0:104, LANES : 2 * LANES]
            tail = field[0:104, 2 * LANES : 3 * LANES]
            half = iota((56, LANES), 1) < LANES // 2
            turned = pltpu.roll(tail, LANES // 2, 1)
            upper = jnp.concatenate([turned[56:104], jnp.zeros((8, LANES), F32)], 0)
            face_msg[0:104] = head
            face_msg[104:160] = jnp.where(half, tail[0:56], upper)
            faces[spot] = face_msg[...]

            @pl.when(sub > 0)
            def _():
                beside(first_src, ends, 1, se, re, sub - 1).start()

        if tile == tiles - 1:

            @pl.when(sub < subs - 1)
            def _():
                beside(last_src, ends, 0, se, re, sub + 1).start()

        pace(3)

    left_s[...] = stacked_left(lhs_s[...], PAD, 4 * LANES)
    row56 = iota((56, width), 0)

    def second(tile):
        cols = slice(tile * width, (tile + 1) * width)
        u = field[:, LANES + tile * width : LANES + (tile + 1) * width]
        su = dot(left_s[:, 0:WIDE], stacked_right(u))
        c_row = coeff[:, cols]
        resid[0:trace] = rhs[:, cols] - su[:trace] * c_row - u[:trace]
        wide = field[96:152, tile * width : (tile + 1) * width + 2 * LANES]
        span = width + 2 * LANES
        below = pltpu.roll(wide, 1, 1)[:, LANES : LANES + width]
        above = pltpu.roll(wide, span - 1, 1)[:, LANES : LANES + width]
        below = pltpu.roll(below, 56 - FACE, 0)
        above = pltpu.roll(above, FACE, 0)
        column = jnp.where(
            (row56 >= 4) & (row56 < 4 + FACE), below,
            jnp.where((row56 >= 4 + FACE) & (row56 < 4 + 2 * FACE), above, 0.0),
        )
        resid[96:152] = resid[96:152] + column
        made = dot(left_m[0:PAD, 0:WIDE], stacked_right(resid[...]))
        out[:, cols] = u[:trace] + made[:trace] * (0.5 / c_row)

    early = [1] if tiles > 2 else []
    for tile in early:
        second(tile)
        pace(len(queue))

    @pl.when(sub > 0)
    def _():
        beside(last_src, ends, 0, se, re, sub - 1).wait_recv()
        field[96:152, 0:LANES] = ends[0]

    @pl.when(sub == 0)
    def _():
        field[96:152, 0:LANES] = jnp.zeros((56, LANES), F32)

    @pl.when(sub < subs - 1)
    def _():
        beside(first_src, ends, 1, se, re, sub + 1).wait_recv()
        field[96:152, LANES + elements : 2 * LANES + elements] = ends[1]

    @pl.when(sub == subs - 1)
    def _():
        field[96:152, LANES + elements : 2 * LANES + elements] = jnp.zeros((56, LANES), F32)

    ends_left = pltpu.roll(
        jnp.concatenate([low_part, high_part], 0), 2 * LANES - 96, 1
    )[:, :56]
    from_ends = jnp.dot(
        ends_left,
        jnp.concatenate(
            [field[96:152, 0:LANES], field[96:152, LANES + elements : 2 * LANES + elements]], 1
        ),
        precision=HIGHEST, preferred_element_type=F32,
    )
    below_last = from_ends[8:16, LANES - 1 : LANES]
    above_first = from_ends[0:8, LANES : LANES + 1]
    next_first = jnp.where(
        lane == nrb - 1, above_first, pltpu.roll(firsts, LANES - 1, 1)
    )
    last_before = jnp.where(lane == 0, below_last, pltpu.roll(lasts, 1, 1))
    msg3[0:8] = place(sums - less - firsts + next_first - lasts + last_before)
    msg3[8:16] = place(side_sums)
    got3[me] = msg3[...]
    spread(msg3, got3, s3, r3)

    collect(msg1, got1, s1, r1)

    def packed(got):
        return [
            jnp.sum(got[t * per_pack : (t + 1) * per_pack], 0) for t in range(packs)
        ]

    first_pack = packed(got1)
    owner_rows = [p[8:9] for p in first_pack]
    eye = iota((LANES, LANES), 0) == iota((LANES, LANES), 1)
    earlier = iota((LANES, LANES), 0) < iota((LANES, LANES), 1)
    owner_cols = [
        jnp.sum(jnp.where(eye, row, 0.0), 1, keepdims=True) for row in owner_rows
    ]
    slot_rows = []
    for t in range(packs):
        slot = jnp.zeros((1, LANES), F32)
        for before in range(t + 1):
            same = owner_cols[before] == owner_rows[t]
            if before == t:
                same = same & earlier
            slot = slot + jnp.sum(jnp.where(same, 1.0, 0.0), 0, keepdims=True)
        slot_rows.append(slot)
    order = COARSE * CAPO
    slot_of = (iota((order, LANES), 0) // COARSE).astype(F32)
    me_real = me.astype(F32)
    chosen = [
        jnp.where((slot_of == slot_rows[t]) & (owner_rows[t] == me_real), 1.0, 0.0).astype(BF16)
        for t in range(packs)
    ]
    pick = lax.rem(iota((order, 2 * COARSE), 0), COARSE) == lax.rem(
        iota((order, 2 * COARSE), 1), COARSE
    )

    def solve(packs_of):
        total = jnp.zeros((order, 2 * COARSE), F32)
        for t in range(packs):
            total = total + nt(chosen[t], jnp.concatenate(halves(packs_of[t]), 0))
        column = jnp.sum(jnp.where(pick, total, 0.0), 1, keepdims=True)
        return jnp.sum(c_inv[...] * column, 0, keepdims=True)

    load_solver.wait()
    y_a[...] = solve([p[0:8] for p in first_pack])
    got_a[me] = y_a[...]
    in_block = lax.rem(lane, nrb)
    keep_eight = iota((COARSE, order), 0) == lax.rem(iota((COARSE, order), 1), COARSE)
    mine = jnp.concatenate(halves(jnp.where(keep_eight, 0.5 * y_a[...], 0.0)), 0)
    for t in range(packs):
        held = dot(mine, chosen[t])
        held = held[0:8] + held[8:16]
        turned = pltpu.roll(
            jnp.where(in_block == nrb - 1, held, 0.0), LANES - (nrb - 1), 1,
            stride=1, stride_axis=0,
        ) + pltpu.roll(jnp.where(in_block == 0, held, 0.0), COARSE, 1, stride=1, stride_axis=0)
        edge[:, t * LANES : (t + 1) * LANES] = jnp.sum(turned, 0, keepdims=True)

    def send_edges(slot, peer_sub):
        def one(j, carry):
            edge_copy(slot, me, every(j), peer_sub).start()
            return carry

        lax.fori_loop(0, blocks, one, 0)

    @pl.when(sub < subs - 1)
    def _():
        send_edges(0, sub + 1)

    @pl.when(sub > 0)
    def _():
        send_edges(1, sub - 1)

    spread(y_a, got_a, s2, r2)

    for tile in range(tiles):
        if tile not in early:
            second(tile)

    unit = jnp.where(iota((PAD, trace), 0) == iota((PAD, trace), 1), 1.0, 0.0)
    r_high = restriction_high = spread_r[:, :trace].astype(BF16).astype(F32)
    r_low = spread_r[:, :trace] - restriction_high
    left_lift = nt(
        unit.astype(BF16), jnp.concatenate([r_high, r_high, r_low], 0).astype(BF16)
    )
    lifted = nt(
        unit.astype(BF16),
        jnp.concatenate([r_high, jnp.zeros((15 * COARSE, trace), F32)], 0).astype(BF16),
    ) + nt(
        unit.astype(BF16),
        jnp.concatenate([r_low, jnp.zeros((15 * COARSE, trace), F32)], 0).astype(BF16),
    )
    left_lift = left_lift.astype(BF16)
    both = lhs[...]
    weights = nt(
        both[:, :trace],
        jnp.concatenate([base[:, :trace], jnp.zeros((8 * COARSE, trace), F32)], 0), HIGHEST,
    )
    signs = jnp.where(iota((PAD, LANES), 1) < 4 * COARSE, -0.5, 0.5)
    rows_in = iota((PAD, LANES), 0) < trace
    correct = jnp.where(rows_in, lifted + weights * signs, 0.0)
    left_wide = stacked_left(correct, 8 * COARSE, 2 * LANES)[:, : 24 * COARSE]
    left_slim = stacked_left(
        jnp.where(iota((PAD, LANES), 1) < 4 * COARSE, correct, 0.0), 4 * COARSE, LANES
    )[:, : 12 * COARSE]
    left_reduced = stacked_left(weights[152:160], 8 * COARSE, 2 * LANES)[:, : 24 * COARSE]

    target = jnp.where(lane < nrb, me * nrb + lane, -1)
    for k in range(4):
        target = jnp.where(lane == nrb + k, partner_s[0, k] * nrb, target)
    pairs = [
        jnp.where(row8 == 0, owner_rows[t] + 1.0, slot_rows[t]).astype(BF16)
        for t in range(packs)
    ]
    own_sel = []
    found = zero_tile
    for t in range(packs):
        sel = iota((LANES, LANES), 0) + t * LANES == target[0:1]
        own_sel.append(jnp.where(sel, 1.0, 0.0).astype(BF16))
        found = found + dot(pairs[t], own_sel[t])
    back_owner, back_slot = found[0:1], found[1:2]
    back = jnp.where(slot_of == back_slot, 1.0, 0.0).astype(BF16)

    lane_row = iota((LANES, LANES), 0)
    def cross(values, extra):
        rows = values[0].shape[0]
        results = []
        for t in range(packs):
            wanted = first_pack[t][9:10] * float(nrb) + extra
            total = jnp.zeros((rows, LANES), F32)
            for source in range(packs):
                sel = (lane_row + source * LANES).astype(F32) == wanted
                total = total + dot(values[source], jnp.where(sel, 1.0, 0.0).astype(BF16))
            results.append(total)
        return results

    crossed_pairs = cross(pairs, 0.0)
    slots_both = [
        jnp.concatenate(
            [
                jnp.where(slot_of == slot_rows[t], 1.0, 0.0),
                jnp.where(slot_of == crossed_pairs[t][1:2], 1.0, 0.0),
            ],
            1,
        ).astype(BF16)
        for t in range(packs)
    ]
    owners_both = [
        jnp.concatenate([owner_rows[t] + 1.0, crossed_pairs[t][0:1]], 1) for t in range(packs)
    ]
    keep_row = (
        iota((blocks, COARSE, order), 1) == lax.rem(iota((blocks, COARSE, order), 2), COARSE)
    )

    def rows_of(got):
        rows = jnp.where(keep_row, got[...], 0.0).reshape(blocks * COARSE, order)
        return jnp.concatenate(halves(rows), 0)

    def fetch(rows, at_slot, owner_row):
        lanes = at_slot.shape[1]
        block_of = iota((blocks, COARSE, lanes), 0).astype(F32) + 1.0
        made = dot(rows, at_slot)
        count = blocks * COARSE
        made = (made[:count] + made[count:]).reshape(blocks, COARSE, lanes)
        return jnp.sum(jnp.where(block_of == owner_row[None], made, 0.0), 0)

    def fold(values):
        total = values
        for k in range(1, 4):
            total = total + pltpu.roll(values, LANES - k, 1)
        return jnp.where(in_block == 0, total, 0.0)

    packed_row = iota((160, LANES), 0)
    face_row = jnp.where(
        packed_row < 104, packed_row,
        jnp.where(iota((160, LANES), 1) < LANES // 2, packed_row - 104, packed_row - 48),
    )

    def sources(of):
        wanted = jnp.full((160, LANES), -1.0, F32)
        for q in range(4):
            inside = (face_row >= q * FACE) & (face_row < (q + 1) * FACE)
            wanted = jnp.where(inside, of[q ^ 1], wanted)
        return wanted

    first_block = (group * QUAD).astype(F32)

    def from_group(wanted):
        taken = jnp.zeros((160, LANES), F32)
        for q in range(QUAD):
            taken = jnp.where(wanted == first_block + float(q), faces[q], taken)
        return taken

    for step in range(1, QUAD):
        whence = lax.rem(spot + step, QUAD)
        face_copy(whence, whence).wait_recv()
    for step in range(1, groups):
        to = lax.rem(group + step, groups)
        wanted = []
        for k in range(4):
            total = jnp.zeros((1, 1), F32)
            for t in range(packs):
                here = lane[0:1] + t * LANES == (to * QUAD + spot) * nrb + k
                total = total + jnp.sum(
                    jnp.where(here, first_pack[t][9:10], 0.0), 1, keepdims=True
                )
            wanted.append(total)
        pass_msg[to] = from_group(sources(wanted))
        pass_copy(group, to).start()

    collect(msg3, got3, s3, r3)
    third_pack = packed(got3)
    swapped = (in_block + 1 - 2 * lax.rem(in_block, 2)).astype(F32)[0:1]
    side_in = cross([jnp.concatenate(halves(p[8:16]), 0) for p in third_pack], swapped)
    base_sums = [
        third_pack[t][0:8] + fold(side_in[t][0:8] + side_in[t][8:16]) for t in range(packs)
    ]

    collect(y_a, got_a, s2, r2)
    rows = rows_of(got_a)
    fetched = [0.5 * fetch(rows, slots_both[t], owners_both[t]) for t in range(packs)]

    def take_edges(slot, peer_sub):
        def one(j, carry):
            edge_copy(slot, lax.rem(me + j, blocks), lax.rem(me + j, blocks), peer_sub).wait_recv()
            return carry

        lax.fori_loop(0, blocks, one, 0)

    @pl.when(sub > 0)
    def _():
        take_edges(0, sub - 1)

    @pl.when(sub == 0)
    def _():
        got_edge[0] = jnp.zeros((blocks, 1, edge_lanes), F32)

    @pl.when(sub < subs - 1)
    def _():
        take_edges(1, sub + 1)

    @pl.when(sub == subs - 1)
    def _():
        got_edge[1] = jnp.zeros((blocks, 1, edge_lanes), F32)

    near = [jnp.sum(got_edge[q], 0) for q in range(2)]
    states = []
    seconds = []
    for t in range(packs):
        omega, crossed = fetched[t][:, :LANES], fetched[t][:, LANES:]
        below, above = (
            jnp.broadcast_to(v[:, t * LANES : (t + 1) * LANES], (COARSE, LANES)) for v in near
        )
        beyond = jnp.where(in_block < COARSE, below, above)
        beyond = jnp.where(lax.rem(in_block, COARSE) == row8, beyond, 0.0)
        for bit in (1, 2, 4):
            beyond = jnp.where((row8 & bit) > 0, pltpu.roll(beyond, LANES - bit, 1), beyond)
        before = jnp.where(in_block == 0, beyond, pltpu.roll(omega, 1, 1))
        after = jnp.where(
            in_block == nrb - 1, pltpu.roll(beyond, nrb - 1 - COARSE, 1),
            pltpu.roll(omega, LANES - 1, 1),
        )
        step_down = omega - before
        step_up = omega - after
        values = [omega * first_pack[t][11:12], float(AGG) * omega, step_down, step_up]
        share = crossed * (-first_pack[t][10:11])
        for k in range(4):
            turned = share if k == 0 else pltpu.roll(share, LANES - k, 1)
            values.append(jnp.where(in_block == 0, turned, 0.0))
        change = dot(left_reduced, stacked_right(jnp.concatenate(values, 0)))
        seconds.append(base_sums[t] - change)
        states.append(jnp.concatenate([omega, step_down, step_up, zero_tile], 0))
    y_b[...] = solve(seconds)
    got_b[me] = y_b[...]
    spread(y_b, got_b, s4, r4)

    state = jnp.zeros((8 * COARSE, LANES), F32)
    for t in range(packs):
        state = state + dot(jnp.concatenate(halves(states[t]), 0), own_sel[t])
    state = state[0:32] + state[32:64]
    omega, step_down, step_up = state[0:8], state[8:16], state[16:24]
    across = [omega[:, nrb + k : nrb + k + 1] for k in range(4)]

    left_lateral = jnp.where(iota((PAD, LANES), 1) < 4 * FACE, lhs[:, 0:LANES], 0.0)
    left_lateral = jnp.where(iota((PAD, LANES), 0) < trace, left_lateral, 0.0)
    high, low = halves(left_lateral)
    left_lateral = jnp.concatenate([high, high, low], 1)

    def lateral_change():
        wanted = sources([partner_s[0, k].astype(F32) for k in range(4)])
        taken = from_group(wanted)
        for step in range(1, groups):
            whence = lax.rem(group + step, groups)
            pass_copy(whence, whence).wait_recv()
            start = (whence * QUAD).astype(F32)
            inside = (wanted >= start) & (wanted < start + float(QUAD))
            taken = jnp.where(inside, passed[whence], taken)
        unfolded = taken[104:160]
        turned = pltpu.roll(unfolded, LANES // 2, 1)
        wide = jnp.concatenate(
            [taken[0:104], jnp.concatenate([unfolded, turned[0:48]], 0)], 1
        )
        backward = pltpu.roll(wide, 104 - FACE, 0)
        forward = pltpu.roll(wide, FACE, 0)
        row = iota((104, 2 * LANES), 0)
        col = iota((104, 2 * LANES), 1)
        lateral = jnp.zeros((104, 2 * LANES), F32)
        for k in range(4):
            inside = (row >= k * FACE) & (row < (k + 1) * FACE) & (col < counts_s[0, k])
            lateral = jnp.where(inside, backward if k % 2 == 0 else forward, lateral)
        lateral = jnp.concatenate([lateral, jnp.zeros((LANES - 104, 2 * LANES), F32)], 0)
        made = dot(left_lateral, stacked_right(lateral))
        out[:, 0 : 2 * LANES] = out[:, 0 : 2 * LANES] + made[:trace] * (
            0.5 / coeff[:, 0 : 2 * LANES]
        )

    wide_lane = iota((COARSE, width), 1)
    step = lax.rem(wide_lane, AGG)

    def spread_lanes(values, tile):
        pieces = []
        for p in range(PER_TILE // 2):
            at = tile * PER_TILE + 2 * p
            even = jnp.broadcast_to(values[:, at : at + 1], (COARSE, LANES))
            odd = jnp.broadcast_to(values[:, at + 1 : at + 2], (COARSE, LANES))
            pieces += [even, jnp.where(left_half, even, odd), odd]
        return jnp.concatenate(pieces, 1)

    def coarse_change(tile):
        cols = slice(tile * width, (tile + 1) * width)
        inverse = 1.0 / coeff[:, cols]
        here = spread_lanes(omega, tile)
        scaled = here * inverse
        down = jnp.where(step == 0, spread_lanes(step_down, tile) * inverse, 0.0)
        up = jnp.where(step == AGG - 1, spread_lanes(step_up, tile) * inverse, 0.0)
        rows = [here, scaled, down, up]
        if tile == 0:
            for k in range(4):
                rows.append(jnp.where(wide_lane < counts_s[0, k], across[k] * inverse, 0.0))
        left = left_wide if tile == 0 else left_slim
        made = dot(left, stacked_right(jnp.concatenate(rows, 0)))
        out[:, cols] = out[:, cols] + made[:trace]

    for tile in range(tiles):
        coarse_change(tile)
    sent(msg1, got1, s1, r1)
    for step in range(1, QUAD):
        face_copy(spot, lax.rem(spot + step, QUAD)).wait_send()
    sent(y_a, got_a, s2, r2)
    sent(msg3, got3, s3, r3)

    def edges_sent(slot, peer_sub):
        def one(j, carry):
            edge_copy(slot, me, lax.rem(me + j, blocks), peer_sub).wait_send()
            return carry

        lax.fori_loop(0, blocks, one, 0)

    @pl.when(sub < subs - 1)
    def _():
        beside(last_src, ends, 0, se, re, sub + 1).wait_send()
        edges_sent(0, sub + 1)

    @pl.when(sub > 0)
    def _():
        beside(first_src, ends, 1, se, re, sub - 1).wait_send()
        edges_sent(1, sub - 1)

    lateral_change()
    for step in range(1, groups):
        pass_copy(group, lax.rem(group + step, groups)).wait_send()

    collect(y_b, got_b, s4, r4)
    final = 0.5 * fetch(rows_of(got_b), back, back_owner)
    high = final.astype(BF16).astype(F32)
    lift_out[...] = dot(
        left_lift, jnp.concatenate([high, final - high, high], 0).astype(BF16)
    )[: lift_out.shape[0]]
    sent(y_b, got_b, s4, r4)


def finish(lift, held, out_hbm, done, store):
    rows, elements = held.shape
    width = 2 * AGG
    tiles = elements // width
    stores = []
    for t in range(tiles):
        cols = pl.ds(t * width, width)
        stores.append(pltpu.make_async_copy(done.at[:, cols], out_hbm.at[:, cols], store.at[t]))
    split = iota((rows, LANES), 1) < LANES // 2
    for t in range(tiles):
        first = jnp.broadcast_to(lift[:rows, 2 * t : 2 * t + 1], (rows, LANES))
        second = jnp.broadcast_to(lift[:rows, 2 * t + 1 : 2 * t + 2], (rows, LANES))
        left, mid, right = (pl.ds(t * width + q * LANES, LANES) for q in range(3))
        done[:, left] = held[:, left] + first
        done[:, mid] = held[:, mid] + jnp.where(split, first, second)
        done[:, right] = held[:, right] + second
        stores[t].start()
    for copy in stores:
        copy.wait()


def per_device(blocks, subs, rhs, coeff, s_ref, m_inv, restriction, partner, counts, owner, c_inv):
    trace, elements = rhs.shape
    width = PER_TILE * AGG
    order = COARSE * CAPO
    vmem = pl.BlockSpec(memory_space=pltpu.VMEM)
    edge_lanes = blocks * owner.shape[2]
    far = pl.BlockSpec(memory_space=pltpu.HBM)
    dma = pltpu.SemaphoreType.DMA
    held, lift = pl.pallas_call(
        functools.partial(kernel, blocks, subs),
        out_shape=(
            pltpu.VMEM((trace, elements), F32),
            pltpu.VMEM((152, LANES), F32),
        ),
        in_specs=[far] * 9,
        out_specs=(vmem, vmem),
        scratch_shapes=[
            pltpu.SMEM((1, 4), jnp.int32),
            pltpu.SMEM((1, 4), jnp.int32),
            pltpu.SMEM((1, owner.shape[2]), jnp.int32),
            pltpu.VMEM((1, elements), F32),
            pltpu.VMEM((trace, trace), F32),
            pltpu.VMEM((trace, trace), F32),
            pltpu.VMEM((COARSE, trace), F32),
            pltpu.VMEM((COARSE, 2 * LANES), F32),
            pltpu.VMEM((trace, elements), F32),
            pltpu.VMEM((2 * PAD, width), BF16),
            pltpu.VMEM((order, order), F32),
            pltpu.VMEM((PAD, 2 * LANES), F32),
            pltpu.VMEM((PAD, 2 * LANES), F32),
            pltpu.VMEM((PAD + 8 * COARSE, 4 * LANES), BF16),
            pltpu.VMEM((PAD, 4 * LANES), BF16),
            pltpu.VMEM((PAD, elements + 2 * LANES), F32),
            pltpu.VMEM((PAD, width), F32),
            pltpu.VMEM((PAD, LANES), F32),
            pltpu.VMEM((16, LANES), F32),
            pltpu.VMEM((16, LANES), F32),
            pltpu.VMEM((blocks, 16, LANES), F32),
            pltpu.VMEM((blocks, 16, LANES), F32),
            pltpu.VMEM((1, order), F32),
            pltpu.VMEM((1, order), F32),
            pltpu.VMEM((blocks, 1, order), F32),
            pltpu.VMEM((blocks, 1, order), F32),
            pltpu.VMEM((1, edge_lanes), F32),
            pltpu.VMEM((2, blocks, 1, edge_lanes), F32),
            pltpu.VMEM((160, LANES), F32),
            pltpu.VMEM((QUAD, 160, LANES), F32),
            pltpu.VMEM((blocks // QUAD, 160, LANES), F32),
            pltpu.VMEM((blocks // QUAD, 160, LANES), F32),
            pltpu.VMEM((2, 56, LANES), F32),
        ]
        + [dma((blocks,))] * 8
        + [dma((2, blocks))] * 2
        + [dma((QUAD,))] * 2
        + [dma((2,))] * 2
        + [dma((blocks // QUAD,))] * 2
        + [dma((elements // width,)), dma, dma((7,))],
        compiler_params=pltpu.CompilerParams(
            collective_id=0, has_side_effects=True
        ),
    )(
        partner, counts[0], owner[0], rhs, coeff[None, :], s_ref, m_inv, restriction, c_inv[0, 0],
    )
    pairs = elements // (2 * AGG)
    return pl.pallas_call(
        finish,
        out_shape=jax.ShapeDtypeStruct((trace, elements), F32),
        in_specs=[vmem, vmem],
        out_specs=far,
        scratch_shapes=[
            pltpu.VMEM((trace, elements), F32),
            dma((pairs,)),
        ],
    )(*[pltpu.with_memory_space_constraint(v, pltpu.VMEM) for v in (lift, held)])


def solution(mesh):
    in_specs = (
        P(None, ("blk", "sub")),
        P(("blk", "sub")),
        P(),
        P(),
        P(),
        P("blk", None),
        P("blk", "sub", None),
        P("blk", "sub", None),
        P("blk", "sub", None, None),
    )
    out_specs = P(None, ("blk", "sub"))
    body = functools.partial(per_device, mesh.shape["blk"], mesh.shape["sub"])
    return jax.shard_map(
        body, mesh=mesh, in_specs=in_specs, out_specs=out_specs, check_vma=False
    )
```

```python
import functools

import jax
import jax.numpy as jnp
from jax import lax
from jax.experimental import pallas as pl
from jax.experimental.pallas import tpu as pltpu
from jax.sharding import PartitionSpec as P

FACE = 25
COARSE = 8
CAP = 192
CAPO = 64
AGG = 192
LANES = 128
PER_TILE = 4
PAD = 160
PIECE = 32
QUAD = 4
WIDE = 3 * PAD
F32 = jnp.float32
BF16 = jnp.bfloat16
HIGHEST = lax.Precision.HIGHEST
MESH = pl.DeviceIdType.MESH


def iota(shape, dim):
    return lax.broadcasted_iota(jnp.int32, shape, dim)


def halves(x):
    high = x.astype(BF16)
    return high, (x - high.astype(F32)).astype(BF16)


def stacked_left(x, block, width):
    rows, lanes = x.shape
    if lanes < width:
        x = jnp.concatenate([x, jnp.zeros((rows, width - lanes), F32)], 1)
    high = x.astype(BF16).astype(F32)
    low = x - high
    return (high + pltpu.roll(high, block, 1) + pltpu.roll(low, 2 * block, 1)).astype(BF16)


def stacked_right(x):
    high, low = halves(x)
    return jnp.concatenate([high, low, high], 0)


def dot(a, b):
    return jnp.dot(a, b, preferred_element_type=F32)


def nt(a, b, precision=None):
    return lax.dot_general(
        a, b, (((1,), (1,)), ((), ())), precision=precision, preferred_element_type=F32
    )


def kernel(
    blocks, subs,
    partner_hbm, counts_hbm, owner_hbm,
    rhs_hbm, coeff_hbm, s_ref_hbm, m_inv_hbm, restriction_hbm, c_inv_hbm,
    out, lift_out,
    partner_s, counts_s, owner_s, coeff, s_ref, m_inv, restriction, rpad,
    rhs, split, c_inv, lhs, lhs_s, left_m, left_s, field, resid, tall, base,
    msg1, msg3, got1, got3, y_a, y_b, got_a, got_b, edge, got_edge,
    face_msg, faces, pass_msg, passed, ends,
    s1, r1, s2, r2, s3, r3, s4, r4, sx, rx, sf, rf, se, re, sp, rp, load, load_c, load_s,
):
    elements = rhs.shape[1]
    trace = m_inv.shape[0]
    nrb = elements // AGG
    width = PER_TILE * AGG
    tiles = elements // width
    packs = blocks * nrb // LANES
    per_pack = LANES // nrb
    edge_lanes = edge.shape[1]
    me = lax.axis_index("blk")
    sub = lax.axis_index("sub")
    has_below = (sub > 0).astype(jnp.int32)
    has_above = (sub < subs - 1).astype(jnp.int32)
    rising = (me * 2 < blocks).astype(jnp.int32)

    def every(j):
        return rising * (blocks - 1 - j) + (1 - rising) * j

    def other(j):
        down = blocks - 1 - j
        down = down - (down <= me).astype(jnp.int32)
        up = j + (j >= me).astype(jnp.int32)
        return rising * down + (1 - rising) * up

    barrier = pltpu.get_barrier_semaphore()

    def greet(j, carry):
        pl.semaphore_signal(barrier, inc=1, device_id={"blk": other(j)}, device_id_type=MESH)
        return carry

    lax.fori_loop(0, blocks - 1, greet, 0)

    @pl.when(sub > 0)
    def _():
        pl.semaphore_signal(barrier, inc=1, device_id={"sub": sub - 1}, device_id_type=MESH)

    @pl.when(sub < subs - 1)
    def _():
        pl.semaphore_signal(barrier, inc=1, device_id={"sub": sub + 1}, device_id_type=MESH)

    small = [
        pltpu.make_async_copy(src, dst, load_s.at[i])
        for i, (src, dst) in enumerate(
            [
                (restriction_hbm, restriction), (owner_hbm, owner_s),
                (partner_hbm, partner_s), (counts_hbm, counts_s), (coeff_hbm, coeff),
                (m_inv_hbm, m_inv), (s_ref_hbm, s_ref),
            ]
        )
    ]
    loads = [
        pltpu.make_async_copy(
            rhs_hbm.at[:, pl.ds(t * width, width)],
            rhs.at[:, pl.ds(t * width, width)], load.at[t],
        )
        for t in range(tiles)
    ]
    load_solver = pltpu.make_async_copy(c_inv_hbm, c_inv, load_c)
    for copy in small[:5] + loads + small[5:]:
        copy.start()
    load_solver.start()

    def spread(src, dst, send, recv):
        def one(j, carry):
            pltpu.make_async_remote_copy(
                src_ref=src, dst_ref=dst.at[me], send_sem=send, recv_sem=recv,
                device_id={"blk": other(j)}, device_id_type=MESH,
            ).start()
            return carry

        lax.fori_loop(0, blocks - 1, one, 0)

    def all_of(dst, send, recv):
        part = dst.at[pl.ds(0, blocks - 1)]
        return pltpu.make_async_remote_copy(
            src_ref=part, dst_ref=part, send_sem=send, recv_sem=recv,
            device_id={"blk": other(0)}, device_id_type=MESH,
        )

    def collect(src, dst, send, recv):
        all_of(dst, send, recv).wait_recv()

    def sent(src, dst, send, recv):
        all_of(dst, send, recv).wait_send()

    def beside(src, dst, slot, send, recv, peer):
        return pltpu.make_async_remote_copy(
            src_ref=src, dst_ref=dst.at[slot], send_sem=send.at[slot], recv_sem=recv.at[slot],
            device_id={"sub": peer}, device_id_type=MESH,
        )

    def edge_copy(slot, peer, peer_sub):
        return pltpu.make_async_remote_copy(
            src_ref=edge, dst_ref=got_edge.at[slot, me], send_sem=sx.at[slot],
            recv_sem=rx.at[slot], device_id={"blk": peer, "sub": peer_sub}, device_id_type=MESH,
        )

    def all_edges(slot, peer_sub):
        return pltpu.make_async_remote_copy(
            src_ref=got_edge.at[slot], dst_ref=got_edge.at[slot], send_sem=sx.at[slot],
            recv_sem=rx.at[slot], device_id={"sub": peer_sub}, device_id_type=MESH,
        )

    lane = iota((COARSE, LANES), 1)
    left_half = lane < LANES // 2
    zero_tile = jnp.zeros((COARSE, LANES), F32)

    def lane_sums(values, total, tile):
        for p in range(PER_TILE // 2):
            first, mid, last = (
                values[:, (3 * p + q) * LANES : (3 * p + q + 1) * LANES] for q in range(3)
            )
            even = first + jnp.where(left_half, mid, 0.0)
            odd = last + jnp.where(left_half, 0.0, mid)
            at = tile * PER_TILE + 2 * p
            total = jnp.where(lane == at, jnp.sum(even, 1, keepdims=True), total)
            total = jnp.where(lane == at + 1, jnp.sum(odd, 1, keepdims=True), total)
        return total

    def lane_picks(values, total, tile, offset):
        for a in range(PER_TILE):
            at = a * AGG + offset
            total = jnp.where(lane == tile * PER_TILE + a, values[:, at : at + 1], total)
        return total

    rpad[...] = jnp.zeros((COARSE, 2 * LANES), F32)
    for row in (0, PAD):
        split[row + trace : row + PAD] = jnp.zeros((PAD - trace, width), BF16)
    resid[trace:PAD] = jnp.zeros((PAD - trace, width), F32)
    tall[trace:PAD] = jnp.zeros((PAD - trace, LANES), F32)
    small[0].wait()
    r_lane = iota((COARSE, 2 * LANES), 1)
    rpad[:, 0:trace] = restriction[...]
    spread_r = rpad[...]
    left_r = stacked_left(spread_r, PAD, 4 * LANES)[:, :WIDE]

    row8 = iota((COARSE, LANES), 0)

    def place(values):
        values = jnp.where(lane < nrb, values, 0.0)
        return pltpu.roll(values, lax.rem(me, per_pack) * nrb, 1)

    def split_tile(cols):
        high, low = halves(rhs[:, cols])
        split[0:trace] = high
        split[PAD : PAD + trace] = low
        high = split[0:PAD]
        return jnp.concatenate([high, split[PAD : 2 * PAD], high], 0)

    def describe():
        coeff_sums = zero_tile
        for tile in range(tiles):
            c_row = jnp.broadcast_to(coeff[:, tile * width : (tile + 1) * width], (COARSE, width))
            coeff_sums = lane_sums(c_row, coeff_sums, tile)
        owner_tile = zero_tile
        for g in range(nrb):
            owner_tile = jnp.where(lane == g, owner_s[0, g].astype(F32), owner_tile)
        for k in range(4):
            owner_tile = jnp.where(
                (row8 == 1) & (lane == k), partner_s[0, k].astype(F32), owner_tile
            )
            owner_tile = jnp.where(
                (row8 == 2) & (lane == k), counts_s[0, k].astype(F32), owner_tile
            )
        owner_tile = jnp.where(row8 == 3, coeff_sums, owner_tile)
        msg1[8:16] = place(owner_tile)

    tall_lane = iota((trace, LANES), 1)
    tall_left = tall_lane < LANES // 2
    totals = jnp.zeros((trace, LANES), F32)
    for tile in range(tiles):
        loads[tile].wait()
        for p in range(PER_TILE // 2):
            first, mid, last = (
                rhs[:, tile * width + (3 * p + q) * LANES : tile * width + (3 * p + q + 1) * LANES]
                for q in range(3)
            )
            even = first + jnp.where(tall_left, mid, 0.0)
            odd = last + jnp.where(tall_left, 0.0, mid)
            at = tile * PER_TILE + 2 * p
            totals = jnp.where(tall_lane == at, jnp.sum(even, 1, keepdims=True), totals)
            totals = jnp.where(tall_lane == at + 1, jnp.sum(odd, 1, keepdims=True), totals)
        if tile == max(tiles - 2, 0):
            for copy in small[1:5]:
                copy.wait()
            describe()
    tall[0:trace] = totals
    sums = dot(left_r, stacked_right(tall[...]))
    msg1[0:8] = place(sums)
    got1[me] = msg1[...]

    backward = pltpu.roll(spread_r, 2 * LANES - FACE, 1)
    forward = pltpu.roll(spread_r, FACE, 1)

    def at_slot(slot, from_slot):
        moved = backward if from_slot > slot else forward
        inside = (r_lane >= slot * FACE) & (r_lane < (slot + 1) * FACE)
        return jnp.where(inside, moved, 0.0)

    low_part, high_part = at_slot(4, 5), at_slot(5, 4)
    sides = [at_slot(k, k ^ 1) for k in range(4)]

    def prepare():
        for copy in small[5:]:
            copy.wait()
        for ref, src in ((lhs, m_inv), (lhs_s, s_ref)):
            ref[...] = jnp.zeros((PAD, 2 * LANES), F32)
            ref[0:trace, 0:trace] = src[...]
        left_m[0:PAD] = stacked_left(lhs[...], PAD, 4 * LANES)
        base[...] = jnp.concatenate(
            [dot(left_r, stacked_right(lhs_s[...]))]
            + [spread_r - low_part - high_part, low_part, high_part] + sides,
            0,
        )
        moved = dot(stacked_left(base[...], PAD, 4 * LANES)[:, :WIDE], stacked_right(lhs[...]))
        left_m[PAD : PAD + 8 * COARSE] = stacked_left(moved, PAD, 4 * LANES)
        left_s[...] = stacked_left(lhs_s[...], PAD, 4 * LANES)
        lhs[152:160] = spread_r

    @pl.when(rising == 1)
    def _():
        prepare()


    pl.semaphore_wait(barrier, blocks - 1 + has_below + has_above)
    spread(msg1, got1, s1, r1)

    @pl.when(rising == 0)
    def _():
        prepare()

    groups = blocks // QUAD
    group = me // QUAD
    spot = lax.rem(me, QUAD)

    def face_copy(place_at, to, rows=slice(None)):
        return pltpu.make_async_remote_copy(
            src_ref=face_msg.at[rows], dst_ref=faces.at[place_at, rows], send_sem=sf.at[to],
            recv_sem=rf.at[place_at], device_id={"blk": group * QUAD + to}, device_id_type=MESH,
        )

    def pass_copy(place_at, to):
        return pltpu.make_async_remote_copy(
            src_ref=pass_msg.at[to], dst_ref=passed.at[place_at], send_sem=sp.at[to],
            recv_sem=rp.at[place_at], device_id={"blk": to * QUAD + spot}, device_id_type=MESH,
        )

    queue = [(step, piece) for piece in range(160 // PIECE) for step in range(1, QUAD)]

    def pace(count):
        for _ in range(min(count, len(queue))):
            step, piece = queue.pop(0)
            rows = pl.ds(piece * PIECE, PIECE)
            face_copy(spot, lax.rem(spot + step, QUAD), rows).start()

    first_src = field.at[96:152, LANES : 2 * LANES]
    last_src = field.at[96:152, elements : elements + LANES]

    less = zero_tile
    firsts = zero_tile
    lasts = zero_tile
    side_sums = zero_tile
    for tile in [0, tiles - 1] + list(range(1, tiles - 1)):
        cols = slice(tile * width, (tile + 1) * width)
        rows = PAD + (8 if tile == 0 else 4) * COARSE
        made = dot(left_m[0:rows, 0:WIDE], split_tile(cols))
        scale = 0.5 / coeff[:, cols]
        field[:, LANES + tile * width : LANES + (tile + 1) * width] = made[:PAD] * scale
        parts = [made[PAD + 8 * i : PAD + 8 * i + 8] for i in range((rows - PAD) // COARSE)]
        less = lane_sums(0.5 * parts[0] + parts[1] * scale, less, tile)
        firsts = lane_picks(parts[2] * scale, firsts, tile, 0)
        lasts = lane_picks(parts[3] * scale, lasts, tile, AGG - 1)
        if tile == 0:
            side_lane = iota((COARSE, 2 * LANES), 1)
            for k in range(4):
                part = parts[4 + k][:, : 2 * LANES] * scale[:, : 2 * LANES]
                part = jnp.where(side_lane < counts_s[0, k], part, 0.0)
                side_sums = jnp.where(lane == k, jnp.sum(part, 1, keepdims=True), side_sums)
            head = field[0:104, LANES : 2 * LANES]
            tail = field[0:104, 2 * LANES : 3 * LANES]
            half = iota((56, LANES), 1) < LANES // 2
            turned = pltpu.roll(tail, LANES // 2, 1)
            upper = jnp.concatenate([turned[56:104], jnp.zeros((8, LANES), F32)], 0)
            face_msg[0:104] = head
            face_msg[104:160] = jnp.where(half, tail[0:56], upper)
            faces[spot] = face_msg[...]

            @pl.when(sub > 0)
            def _():
                beside(first_src, ends, 1, se, re, sub - 1).start()

        if tile == tiles - 1:

            @pl.when(sub < subs - 1)
            def _():
                beside(last_src, ends, 0, se, re, sub + 1).start()

        pace(3)

    row56 = iota((56, width), 0)

    def second(tile):
        cols = slice(tile * width, (tile + 1) * width)
        u = field[:, LANES + tile * width : LANES + (tile + 1) * width]
        su = dot(left_s[:, 0:WIDE], stacked_right(u))
        c_row = coeff[:, cols]
        resid[0:trace] = rhs[:, cols] - su[:trace] * c_row - u[:trace]
        wide = field[96:152, tile * width : (tile + 1) * width + 2 * LANES]
        span = width + 2 * LANES
        below = pltpu.roll(wide, 1, 1)[:, LANES : LANES + width]
        above = pltpu.roll(wide, span - 1, 1)[:, LANES : LANES + width]
        below = pltpu.roll(below, 56 - FACE, 0)
        above = pltpu.roll(above, FACE, 0)
        column = jnp.where(
            (row56 >= 4) & (row56 < 4 + FACE), below,
            jnp.where((row56 >= 4 + FACE) & (row56 < 4 + 2 * FACE), above, 0.0),
        )
        resid[96:152] = resid[96:152] + column
        made = dot(left_m[0:PAD, 0:WIDE], stacked_right(resid[...]))
        out[:, cols] = u[:trace] + made[:trace] * (0.5 / c_row)

    early = [1] if tiles > 2 else []
    for tile in early:
        second(tile)
        pace(len(queue))

    def send_third():
        @pl.when(sub > 0)
        def _():
            beside(last_src, ends, 0, se, re, sub - 1).wait_recv()
            field[96:152, 0:LANES] = ends[0]

        @pl.when(sub == 0)
        def _():
            field[96:152, 0:LANES] = jnp.zeros((56, LANES), F32)

        @pl.when(sub < subs - 1)
        def _():
            beside(first_src, ends, 1, se, re, sub + 1).wait_recv()
            field[96:152, LANES + elements : 2 * LANES + elements] = ends[1]

        @pl.when(sub == subs - 1)
        def _():
            field[96:152, LANES + elements : 2 * LANES + elements] = jnp.zeros((56, LANES), F32)

        ends_left = pltpu.roll(
            jnp.concatenate([low_part, high_part], 0), 2 * LANES - 96, 1
        )[:, :56]
        from_ends = jnp.dot(
            ends_left,
            jnp.concatenate(
                [field[96:152, 0:LANES], field[96:152, LANES + elements : 2 * LANES + elements]], 1
            ),
            precision=HIGHEST, preferred_element_type=F32,
        )
        below_last = from_ends[8:16, LANES - 1 : LANES]
        above_first = from_ends[0:8, LANES : LANES + 1]
        next_first = jnp.where(
            lane == nrb - 1, above_first, pltpu.roll(firsts, LANES - 1, 1)
        )
        last_before = jnp.where(lane == 0, below_last, pltpu.roll(lasts, 1, 1))
        msg3[0:8] = place(sums - less - firsts + next_first - lasts + last_before)
        msg3[8:16] = place(side_sums)
        got3[me] = msg3[...]
        spread(msg3, got3, s3, r3)

    @pl.when(lax.rem(sub, 2) == 0)
    def _():
        send_third()

    collect(msg1, got1, s1, r1)

    def packed(got):
        return [
            jnp.sum(got[t * per_pack : (t + 1) * per_pack], 0) for t in range(packs)
        ]

    first_pack = packed(got1)
    owner_rows = [p[8:9] for p in first_pack]
    eye = iota((LANES, LANES), 0) == iota((LANES, LANES), 1)
    earlier = iota((LANES, LANES), 0) < iota((LANES, LANES), 1)
    owner_cols = [
        jnp.sum(jnp.where(eye, row, 0.0), 1, keepdims=True) for row in owner_rows
    ]
    slot_rows = []
    for t in range(packs):
        slot = jnp.zeros((1, LANES), F32)
        for before in range(t + 1):
            same = owner_cols[before] == owner_rows[t]
            if before == t:
                same = same & earlier
            slot = slot + jnp.sum(jnp.where(same, 1.0, 0.0), 0, keepdims=True)
        slot_rows.append(slot)
    order = COARSE * CAPO
    slot_of = (iota((order, LANES), 0) // COARSE).astype(F32)
    me_real = me.astype(F32)
    chosen = [
        jnp.where((slot_of == slot_rows[t]) & (owner_rows[t] == me_real), 1.0, 0.0).astype(BF16)
        for t in range(packs)
    ]
    pick = lax.rem(iota((order, 2 * COARSE), 0), COARSE) == lax.rem(
        iota((order, 2 * COARSE), 1), COARSE
    )

    def solve(packs_of):
        total = jnp.zeros((order, 2 * COARSE), F32)
        for t in range(packs):
            total = total + nt(chosen[t], jnp.concatenate(halves(packs_of[t]), 0))
        column = jnp.sum(jnp.where(pick, total, 0.0), 1, keepdims=True)
        return jnp.sum(c_inv[...] * column, 0, keepdims=True)

    load_solver.wait()
    y_a[...] = solve([p[0:8] for p in first_pack])
    got_a[me] = y_a[...]
    spread(y_a, got_a, s2, r2)

    in_block = lax.rem(lane, nrb)
    keep_eight = iota((COARSE, order), 0) == lax.rem(iota((COARSE, order), 1), COARSE)
    mine = jnp.concatenate(halves(jnp.where(keep_eight, 0.5 * y_a[...], 0.0)), 0)
    for t in range(packs):
        held = dot(mine, chosen[t])
        held = held[0:8] + held[8:16]
        turned = pltpu.roll(
            jnp.where(in_block == nrb - 1, held, 0.0), LANES - (nrb - 1), 1,
            stride=1, stride_axis=0,
        ) + pltpu.roll(jnp.where(in_block == 0, held, 0.0), COARSE, 1, stride=1, stride_axis=0)
        edge[:, t * LANES : (t + 1) * LANES] = jnp.sum(turned, 0, keepdims=True)

    def send_edges(slot, peer_sub):
        def one(j, carry):
            edge_copy(slot, every(j), peer_sub).start()
            return carry

        lax.fori_loop(0, blocks, one, 0)

    @pl.when(sub < subs - 1)
    def _():
        send_edges(0, sub + 1)

    @pl.when(sub > 0)
    def _():
        send_edges(1, sub - 1)

    @pl.when(lax.rem(sub, 2) == 1)
    def _():
        send_third()

    for tile in range(tiles):
        if tile not in early:
            second(tile)

    packed_row = iota((160, LANES), 0)
    face_row = jnp.where(
        packed_row < 104, packed_row,
        jnp.where(iota((160, LANES), 1) < LANES // 2, packed_row - 104, packed_row - 48),
    )

    def sources(of):
        wanted = jnp.full((160, LANES), -1.0, F32)
        for q in range(4):
            inside = (face_row >= q * FACE) & (face_row < (q + 1) * FACE)
            wanted = jnp.where(inside, of[q ^ 1], wanted)
        return wanted

    first_block = (group * QUAD).astype(F32)

    def from_group(wanted):
        taken = jnp.zeros((160, LANES), F32)
        for q in range(QUAD):
            taken = jnp.where(wanted == first_block + float(q), faces[q], taken)
        return taken

    for step in range(1, QUAD):
        whence = lax.rem(spot + step, QUAD)
        face_copy(whence, whence).wait_recv()
    for step in range(1, groups):
        to = lax.rem(group + step, groups)
        wanted = []
        for k in range(4):
            total = jnp.zeros((1, 1), F32)
            for t in range(packs):
                here = lane[0:1] + t * LANES == (to * QUAD + spot) * nrb + k
                total = total + jnp.sum(
                    jnp.where(here, first_pack[t][9:10], 0.0), 1, keepdims=True
                )
            wanted.append(total)
        pass_msg[to] = from_group(sources(wanted))
        pass_copy(group, to).start()

    unit = jnp.where(iota((PAD, trace), 0) == iota((PAD, trace), 1), 1.0, 0.0)
    r_high = restriction_high = spread_r[:, :trace].astype(BF16).astype(F32)
    r_low = spread_r[:, :trace] - restriction_high
    left_lift = nt(
        unit.astype(BF16), jnp.concatenate([r_high, r_high, r_low], 0).astype(BF16)
    )
    lifted = nt(
        unit.astype(BF16),
        jnp.concatenate([r_high, jnp.zeros((15 * COARSE, trace), F32)], 0).astype(BF16),
    ) + nt(
        unit.astype(BF16),
        jnp.concatenate([r_low, jnp.zeros((15 * COARSE, trace), F32)], 0).astype(BF16),
    )
    left_lift = left_lift.astype(BF16)
    both = lhs[...]
    weights = nt(
        both[:, :trace],
        jnp.concatenate([base[:, 0:trace], jnp.zeros((8 * COARSE, trace), F32)], 0), HIGHEST,
    )
    signs = jnp.where(iota((PAD, LANES), 1) < 4 * COARSE, -0.5, 0.5)
    rows_in = iota((PAD, LANES), 0) < trace
    correct = jnp.where(rows_in, lifted + weights * signs, 0.0)
    left_wide = stacked_left(correct, 8 * COARSE, 2 * LANES)[:, : 24 * COARSE]
    left_slim = stacked_left(
        jnp.where(iota((PAD, LANES), 1) < 4 * COARSE, correct, 0.0), 4 * COARSE, LANES
    )[:, : 12 * COARSE]
    left_reduced = stacked_left(weights[152:160], 8 * COARSE, 2 * LANES)[:, : 24 * COARSE]

    target = jnp.where(lane < nrb, me * nrb + lane, -1)
    for k in range(4):
        target = jnp.where(lane == nrb + k, partner_s[0, k] * nrb, target)
    pairs = [
        jnp.where(row8 == 0, owner_rows[t] + 1.0, slot_rows[t]).astype(BF16)
        for t in range(packs)
    ]
    own_sel = []
    found = zero_tile
    for t in range(packs):
        sel = iota((LANES, LANES), 0) + t * LANES == target[0:1]
        own_sel.append(jnp.where(sel, 1.0, 0.0).astype(BF16))
        found = found + dot(pairs[t], own_sel[t])
    back_owner, back_slot = found[0:1], found[1:2]
    back = jnp.where(slot_of == back_slot, 1.0, 0.0).astype(BF16)

    lane_row = iota((LANES, LANES), 0)
    def cross(values, extra):
        rows = values[0].shape[0]
        results = []
        for t in range(packs):
            wanted = first_pack[t][9:10] * float(nrb) + extra
            total = jnp.zeros((rows, LANES), F32)
            for source in range(packs):
                sel = (lane_row + source * LANES).astype(F32) == wanted
                total = total + dot(values[source], jnp.where(sel, 1.0, 0.0).astype(BF16))
            results.append(total)
        return results

    crossed_pairs = cross(pairs, 0.0)
    slots_both = [
        jnp.concatenate(
            [
                jnp.where(slot_of == slot_rows[t], 1.0, 0.0),
                jnp.where(slot_of == crossed_pairs[t][1:2], 1.0, 0.0),
            ],
            1,
        ).astype(BF16)
        for t in range(packs)
    ]
    owners_both = [
        jnp.concatenate([owner_rows[t] + 1.0, crossed_pairs[t][0:1]], 1) for t in range(packs)
    ]
    keep_row = (
        iota((blocks, COARSE, order), 1) == lax.rem(iota((blocks, COARSE, order), 2), COARSE)
    )

    def rows_of(got):
        rows = jnp.where(keep_row, got[...], 0.0).reshape(blocks * COARSE, order)
        return jnp.concatenate(halves(rows), 0)

    def fetch(rows, at_slot, owner_row):
        lanes = at_slot.shape[1]
        block_of = iota((blocks, COARSE, lanes), 0).astype(F32) + 1.0
        made = dot(rows, at_slot)
        count = blocks * COARSE
        made = (made[:count] + made[count:]).reshape(blocks, COARSE, lanes)
        return jnp.sum(jnp.where(block_of == owner_row[None], made, 0.0), 0)

    def fold(values):
        total = values
        for k in range(1, 4):
            total = total + pltpu.roll(values, LANES - k, 1)
        return jnp.where(in_block == 0, total, 0.0)

    collect(msg3, got3, s3, r3)
    third_pack = packed(got3)
    swapped = (in_block + 1 - 2 * lax.rem(in_block, 2)).astype(F32)[0:1]
    side_in = cross([jnp.concatenate(halves(p[8:16]), 0) for p in third_pack], swapped)
    base_sums = [
        third_pack[t][0:8] + fold(side_in[t][0:8] + side_in[t][8:16]) for t in range(packs)
    ]

    collect(y_a, got_a, s2, r2)
    rows = rows_of(got_a)
    fetched = [0.5 * fetch(rows, slots_both[t], owners_both[t]) for t in range(packs)]

    def take_edges(slot, peer_sub):
        all_edges(slot, peer_sub).wait_recv()

    @pl.when(sub > 0)
    def _():
        take_edges(0, sub - 1)

    @pl.when(sub == 0)
    def _():
        got_edge[0] = jnp.zeros((blocks, 1, edge_lanes), F32)

    @pl.when(sub < subs - 1)
    def _():
        take_edges(1, sub + 1)

    @pl.when(sub == subs - 1)
    def _():
        got_edge[1] = jnp.zeros((blocks, 1, edge_lanes), F32)

    near = [jnp.sum(got_edge[q], 0) for q in range(2)]
    states = []
    seconds = []
    for t in range(packs):
        omega, crossed = fetched[t][:, :LANES], fetched[t][:, LANES:]
        below, above = (
            jnp.broadcast_to(v[:, t * LANES : (t + 1) * LANES], (COARSE, LANES)) for v in near
        )
        beyond = jnp.where(in_block < COARSE, below, above)
        beyond = jnp.where(lax.rem(in_block, COARSE) == row8, beyond, 0.0)
        for bit in (1, 2, 4):
            beyond = jnp.where((row8 & bit) > 0, pltpu.roll(beyond, LANES - bit, 1), beyond)
        before = jnp.where(in_block == 0, beyond, pltpu.roll(omega, 1, 1))
        after = jnp.where(
            in_block == nrb - 1, pltpu.roll(beyond, nrb - 1 - COARSE, 1),
            pltpu.roll(omega, LANES - 1, 1),
        )
        step_down = omega - before
        step_up = omega - after
        values = [omega * first_pack[t][11:12], float(AGG) * omega, step_down, step_up]
        share = crossed * (-first_pack[t][10:11])
        for k in range(4):
            turned = share if k == 0 else pltpu.roll(share, LANES - k, 1)
            values.append(jnp.where(in_block == 0, turned, 0.0))
        change = dot(left_reduced, stacked_right(jnp.concatenate(values, 0)))
        seconds.append(base_sums[t] - change)
        states.append(jnp.concatenate([omega, step_down, step_up, zero_tile], 0))
    y_b[...] = solve(seconds)
    got_b[me] = y_b[...]
    spread(y_b, got_b, s4, r4)

    state = jnp.zeros((8 * COARSE, LANES), F32)
    for t in range(packs):
        state = state + dot(jnp.concatenate(halves(states[t]), 0), own_sel[t])
    state = state[0:32] + state[32:64]
    omega, step_down, step_up = state[0:8], state[8:16], state[16:24]
    across = [omega[:, nrb + k : nrb + k + 1] for k in range(4)]

    left_lateral = jnp.where(iota((PAD, LANES), 1) < 4 * FACE, lhs[:, 0:LANES], 0.0)
    left_lateral = jnp.where(iota((PAD, LANES), 0) < trace, left_lateral, 0.0)
    high, low = halves(left_lateral)
    left_lateral = jnp.concatenate([high, high, low], 1)

    def lateral_change():
        wanted = sources([partner_s[0, k].astype(F32) for k in range(4)])
        taken = from_group(wanted)
        for step in range(1, groups):
            whence = lax.rem(group + step, groups)
            pass_copy(whence, whence).wait_recv()
            start = (whence * QUAD).astype(F32)
            inside = (wanted >= start) & (wanted < start + float(QUAD))
            taken = jnp.where(inside, passed[whence], taken)
        unfolded = taken[104:160]
        turned = pltpu.roll(unfolded, LANES // 2, 1)
        wide = jnp.concatenate(
            [taken[0:104], jnp.concatenate([unfolded, turned[0:48]], 0)], 1
        )
        backward = pltpu.roll(wide, 104 - FACE, 0)
        forward = pltpu.roll(wide, FACE, 0)
        row = iota((104, 2 * LANES), 0)
        col = iota((104, 2 * LANES), 1)
        lateral = jnp.zeros((104, 2 * LANES), F32)
        for k in range(4):
            inside = (row >= k * FACE) & (row < (k + 1) * FACE) & (col < counts_s[0, k])
            lateral = jnp.where(inside, backward if k % 2 == 0 else forward, lateral)
        lateral = jnp.concatenate([lateral, jnp.zeros((LANES - 104, 2 * LANES), F32)], 0)
        made = dot(left_lateral, stacked_right(lateral))
        out[:, 0 : 2 * LANES] = out[:, 0 : 2 * LANES] + made[:trace] * (
            0.5 / coeff[:, 0 : 2 * LANES]
        )

    wide_lane = iota((COARSE, width), 1)
    step = lax.rem(wide_lane, AGG)

    def spread_lanes(values, tile):
        pieces = []
        for p in range(PER_TILE // 2):
            at = tile * PER_TILE + 2 * p
            even = jnp.broadcast_to(values[:, at : at + 1], (COARSE, LANES))
            odd = jnp.broadcast_to(values[:, at + 1 : at + 2], (COARSE, LANES))
            pieces += [even, jnp.where(left_half, even, odd), odd]
        return jnp.concatenate(pieces, 1)

    def coarse_change(tile):
        cols = slice(tile * width, (tile + 1) * width)
        inverse = 1.0 / coeff[:, cols]
        here = spread_lanes(omega, tile)
        scaled = here * inverse
        down = jnp.where(step == 0, spread_lanes(step_down, tile) * inverse, 0.0)
        up = jnp.where(step == AGG - 1, spread_lanes(step_up, tile) * inverse, 0.0)
        rows = [here, scaled, down, up]
        if tile == 0:
            for k in range(4):
                rows.append(jnp.where(wide_lane < counts_s[0, k], across[k] * inverse, 0.0))
        left = left_wide if tile == 0 else left_slim
        made = dot(left, stacked_right(jnp.concatenate(rows, 0)))
        out[:, cols] = out[:, cols] + made[:trace]

    for tile in range(tiles):
        coarse_change(tile)
    sent(msg1, got1, s1, r1)
    for step in range(1, QUAD):
        face_copy(spot, lax.rem(spot + step, QUAD)).wait_send()
    sent(y_a, got_a, s2, r2)
    sent(msg3, got3, s3, r3)

    def edges_sent(slot, peer_sub):
        all_edges(slot, peer_sub).wait_send()

    @pl.when(sub < subs - 1)
    def _():
        beside(last_src, ends, 0, se, re, sub + 1).wait_send()
        edges_sent(0, sub + 1)

    @pl.when(sub > 0)
    def _():
        beside(first_src, ends, 1, se, re, sub - 1).wait_send()
        edges_sent(1, sub - 1)

    lateral_change()
    for step in range(1, groups):
        pass_copy(group, lax.rem(group + step, groups)).wait_send()

    collect(y_b, got_b, s4, r4)
    final = 0.5 * fetch(rows_of(got_b), back, back_owner)
    high = final.astype(BF16).astype(F32)
    lift_out[...] = dot(
        left_lift, jnp.concatenate([high, final - high, high], 0).astype(BF16)
    )[: lift_out.shape[0]]
    sent(y_b, got_b, s4, r4)


def finish(lift, held, out_hbm, done, store):
    rows, elements = held.shape
    width = 2 * AGG
    tiles = elements // width
    stores = []
    for t in range(tiles):
        cols = pl.ds(t * width, width)
        stores.append(pltpu.make_async_copy(done.at[:, cols], out_hbm.at[:, cols], store.at[t]))
    split = iota((rows, LANES), 1) < LANES // 2
    for t in range(tiles):
        first = jnp.broadcast_to(lift[:rows, 2 * t : 2 * t + 1], (rows, LANES))
        second = jnp.broadcast_to(lift[:rows, 2 * t + 1 : 2 * t + 2], (rows, LANES))
        left, mid, right = (pl.ds(t * width + q * LANES, LANES) for q in range(3))
        done[:, left] = held[:, left] + first
        done[:, mid] = held[:, mid] + jnp.where(split, first, second)
        done[:, right] = held[:, right] + second
        stores[t].start()
    for copy in stores:
        copy.wait()


def per_device(blocks, subs, rhs, coeff, s_ref, m_inv, restriction, partner, counts, owner, c_inv):
    trace, elements = rhs.shape
    width = PER_TILE * AGG
    order = COARSE * CAPO
    vmem = pl.BlockSpec(memory_space=pltpu.VMEM)
    edge_lanes = blocks * owner.shape[2]
    far = pl.BlockSpec(memory_space=pltpu.HBM)
    dma = pltpu.SemaphoreType.DMA
    held, lift = pl.pallas_call(
        functools.partial(kernel, blocks, subs),
        out_shape=(
            pltpu.VMEM((trace, elements), F32),
            pltpu.VMEM((152, LANES), F32),
        ),
        in_specs=[far] * 9,
        out_specs=(vmem, vmem),
        scratch_shapes=[
            pltpu.SMEM((1, 4), jnp.int32),
            pltpu.SMEM((1, 4), jnp.int32),
            pltpu.SMEM((1, owner.shape[2]), jnp.int32),
            pltpu.VMEM((1, elements), F32),
            pltpu.VMEM((trace, trace), F32),
            pltpu.VMEM((trace, trace), F32),
            pltpu.VMEM((COARSE, trace), F32),
            pltpu.VMEM((COARSE, 2 * LANES), F32),
            pltpu.VMEM((trace, elements), F32),
            pltpu.VMEM((2 * PAD, width), BF16),
            pltpu.VMEM((order, order), F32),
            pltpu.VMEM((PAD, 2 * LANES), F32),
            pltpu.VMEM((PAD, 2 * LANES), F32),
            pltpu.VMEM((PAD + 8 * COARSE, 4 * LANES), BF16),
            pltpu.VMEM((PAD, 4 * LANES), BF16),
            pltpu.VMEM((PAD, elements + 2 * LANES), F32),
            pltpu.VMEM((PAD, width), F32),
            pltpu.VMEM((PAD, LANES), F32),
            pltpu.VMEM((8 * COARSE, 2 * LANES), F32),
            pltpu.VMEM((16, LANES), F32),
            pltpu.VMEM((16, LANES), F32),
            pltpu.VMEM((blocks, 16, LANES), F32),
            pltpu.VMEM((blocks, 16, LANES), F32),
            pltpu.VMEM((1, order), F32),
            pltpu.VMEM((1, order), F32),
            pltpu.VMEM((blocks, 1, order), F32),
            pltpu.VMEM((blocks, 1, order), F32),
            pltpu.VMEM((1, edge_lanes), F32),
            pltpu.VMEM((2, blocks, 1, edge_lanes), F32),
            pltpu.VMEM((160, LANES), F32),
            pltpu.VMEM((QUAD, 160, LANES), F32),
            pltpu.VMEM((blocks // QUAD, 160, LANES), F32),
            pltpu.VMEM((blocks // QUAD, 160, LANES), F32),
            pltpu.VMEM((2, 56, LANES), F32),
        ]
        + [dma] * 8
        + [dma((2,))] * 2
        + [dma((QUAD,))] * 2
        + [dma((2,))] * 2
        + [dma((blocks // QUAD,))] * 2
        + [dma((elements // width,)), dma, dma((7,))],
        compiler_params=pltpu.CompilerParams(
            collective_id=0, has_side_effects=True
        ),
    )(
        partner, counts[0], owner[0], rhs, coeff[None, :], s_ref, m_inv, restriction, c_inv[0, 0],
    )
    pairs = elements // (2 * AGG)
    return pl.pallas_call(
        finish,
        out_shape=jax.ShapeDtypeStruct((trace, elements), F32),
        in_specs=[vmem, vmem],
        out_specs=far,
        scratch_shapes=[
            pltpu.VMEM((trace, elements), F32),
            dma((pairs,)),
        ],
    )(*[pltpu.with_memory_space_constraint(v, pltpu.VMEM) for v in (lift, held)])


def solution(mesh):
    in_specs = (
        P(None, ("blk", "sub")),
        P(("blk", "sub")),
        P(),
        P(),
        P(),
        P("blk", None),
        P("blk", "sub", None),
        P("blk", "sub", None),
        P("blk", "sub", None, None),
    )
    out_specs = P(None, ("blk", "sub"))
    body = functools.partial(per_device, mesh.shape["blk"], mesh.shape["sub"])
    return jax.shard_map(
        body, mesh=mesh, in_specs=in_specs, out_specs=out_specs, check_vma=False
    )
```
